256 devices in a mesh: grp: 2 (over core), seq: 32 (over y, z), tp: 4 (over x).
Axes of the slice: x: 4, y: 4, z: 8, core: 2. Of those that a mesh axis runs over, the one named last changes fastest.
Arguments:
- patches_in: bfloat16 [65536, 1280], P(('grp', 'seq')), may hold values from -6 to 6
- gain_attn: float32 [1280], replicated, may hold values from 0.25 to 1.75
- gain_merge: float32 [1280], replicated, may hold values from 0.25 to 1.75
- qkv_weight: bfloat16 [1280, 3840], P(None, 'tp'), may hold values from -0.15625 to 0.15625
- out_weight: bfloat16 [1280, 1280], P('tp'), may hold values from -0.15625 to 0.15625
- cotangent: bfloat16 [16384, 5120], P(('grp', 'seq'), 'tp'), may hold values from -0.29882812 to 0.29882812
- patch_counts: int32 [256], P(('grp', 'seq')), may hold values from 64 to 256, as said below
- block_target: int32 [8192], P(('grp', 'seq')), may hold values from 0 to 8191, as said below
Outputs:
- image_rows: bfloat16 [16384, 5120], P(('grp', 'seq'), 'tp')
- grad_qkv: float32 [1280, 3840], P(('grp', 'seq'), 'tp')
- grad_out: float32 [1280, 1280], P('tp', ('grp', 'seq'))
The draws below stay inside these ranges and needn't reach their ends.
Inputs may be any that keep to these rules, and one draw needn't show every extreme that they name: `patch_counts`: multiples of 4; some image has 256 patches in every draw. `block_target`: each sequence block is named exactly once; the 128 blocks of one owner name exactly 2 blocks of each sequence shard (shard = value // 128).
All inputs are finite; a program needn't handle non-finite values.
Results may differ from the reference program's by a relative error of at most 0.02.
Values may be sent and summed in bfloat16 or wider, within the bound.
A program may use at most 128 MiB of HBM per device.

```python
import jax
import jax.numpy as jnp
from jax import lax

DV = 1280
HEAD_V = 80
PATCH_MAX = 256
BROWS = 2
OWNERS = 64
IMAGES = 256
PATCHES = 65536
BLK_DEV = 128
CAPB = 2
BLOCKS = 8192
SEQ_ROWS = 16384


def draw_patch_counts(key, part):
    first_key, second_key = jax.random.split(jax.random.fold_in(key, 11))
    base = jax.random.randint(first_key, (IMAGES,), PATCH_MAX // 16, PATCH_MAX // 4 + 1) * 4
    chosen = jax.random.randint(second_key, (), 0, IMAGES)
    return jnp.where(jnp.arange(IMAGES) == chosen, PATCH_MAX, base).astype(jnp.int32)


def draw_block_target(key, part):
    first_key, second_key = jax.random.split(jax.random.fold_in(key, 23))
    sender_perm = jax.vmap(lambda inner: jax.random.permutation(inner, BLK_DEV))(jax.random.split(first_key, OWNERS))
    shard = sender_perm // CAPB
    within = sender_perm % CAPB
    shard_perm = jax.vmap(lambda inner: jax.random.permutation(inner, BLK_DEV))(jax.random.split(second_key, OWNERS))
    arrival = jnp.arange(OWNERS)[:, None] * CAPB + within
    slot_ids = shard_perm[shard, arrival]
    return (shard * BLK_DEV + slot_ids).reshape(BLOCKS).astype(jnp.int32)


def levels(key, dims, cuts, low, high):
    def one(position, parts):
        heights = jax.random.uniform(jax.random.fold_in(jax.random.fold_in(key, 6), position), (parts,), jnp.float32, low / len(cuts), high / len(cuts))
        return jnp.repeat(jnp.exp(heights), dims[position] // parts).reshape((-1,) + (1,) * (len(dims) - position - 1))

    level = one(*cuts[0])
    for cut in cuts[1:]:
        level = level * one(*cut)
    return level


def bell_draw(key, extent, width, reach, cuts=(), kind=jnp.bfloat16):
    array = width * jax.random.normal(key, extent, jnp.float32)
    if cuts:
        array = array * levels(key, extent, cuts, -0.22, 0.18)
    return jnp.clip(array, -reach, reach).astype(kind)


def setup_inputs(seed: int = 0) -> dict:
    keys = jax.random.split(jax.random.key(seed), 9)
    return {
        "patches_in": bell_draw(keys[0], (PATCHES, DV), 1.0, 6.0, ((0, 64),)),
        "gain_attn": jnp.clip(1.0 + 0.15 * jax.random.normal(keys[1], (DV,), jnp.float32), 0.25, 1.75),
        "gain_merge": jnp.clip(1.0 + 0.15 * jax.random.normal(keys[2], (DV,), jnp.float32), 0.25, 1.75),
        "qkv_weight": bell_draw(keys[3], (DV, 3 * DV), DV ** -0.5, 0.15625, ((1, 4),)),
        "out_weight": bell_draw(keys[4], (DV, DV), DV ** -0.5, 0.15625, ((0, 4),)),
        "cotangent": bell_draw(keys[5], (SEQ_ROWS, 4 * DV), 0.05, 0.29882812, ((0, 64), (1, 4))),
        "patch_counts": draw_patch_counts(jax.random.fold_in(keys[8], 71), 0),
        "block_target": draw_block_target(jax.random.fold_in(keys[8], 71), 0),
    }


def layer_norm(values, gain):
    center = values - lax.optimization_barrier(jnp.mean(values, axis=-1, keepdims=True))
    spread = lax.optimization_barrier(jnp.mean(center * center, axis=-1, keepdims=True))
    return center * lax.rsqrt(spread + 1e-06) * gain.astype(jnp.float32)

def attend(qkv_rows, count):
    length = qkv_rows.shape[0]
    heads_here = qkv_rows.shape[1] // (3 * HEAD_V)
    split_heads = qkv_rows.reshape(length, heads_here, 3, HEAD_V)
    queries = split_heads[:, :, 0]
    keys_all = split_heads[:, :, 1]
    values_all = split_heads[:, :, 2]
    scores = jnp.einsum('qhd,khd->hqk', queries, keys_all, preferred_element_type=jnp.float32) * HEAD_V ** (-0.5)
    key_live = jnp.arange(length) < count
    scores = jnp.where(key_live[None, None, :], scores, -1e+30)
    scores = scores - lax.optimization_barrier(jnp.max(scores, axis=-1, keepdims=True))
    weights = jnp.exp(scores)
    weights = (weights / lax.optimization_barrier(jnp.sum(weights, axis=-1, keepdims=True))).astype(jnp.bfloat16)
    mixed = jnp.einsum('hqk,khd->qhd', weights, values_all, preferred_element_type=jnp.float32)
    return mixed.reshape(length, heads_here * HEAD_V).astype(jnp.bfloat16)

def attend_back(qkv_rows, count, grad_heads):
    pull_back = jax.vjp(lambda inner: attend(inner, count), qkv_rows)[1]
    return pull_back(grad_heads)[0]

def reference(patches_in, gain_attn, gain_merge, qkv_weight, out_weight, cotangent, patch_counts, block_target):
    normed = layer_norm(patches_in.astype(jnp.float32), gain_attn).astype(jnp.bfloat16)
    qkv_rows = jnp.dot(normed, qkv_weight, preferred_element_type=jnp.float32).astype(jnp.bfloat16)
    per_image = qkv_rows.reshape(IMAGES, PATCH_MAX, 3 * DV)
    head_out = lax.map(lambda pair: attend(pair[0], pair[1]), (per_image, patch_counts)).reshape(PATCHES, DV)
    attn_sum = jnp.dot(head_out, out_weight, preferred_element_type=jnp.float32)
    residual = patches_in.astype(jnp.float32) + attn_sum
    live_rows = (jnp.arange(PATCH_MAX)[None, :] < patch_counts[:, None]).reshape(PATCHES, 1).astype(jnp.float32)

    def merge_norm(inner):
        return layer_norm(inner, gain_merge) * live_rows
    merged, pull_back = jax.vjp(merge_norm, residual)
    merged = merged.astype(jnp.bfloat16)
    blocks_all = merged.reshape(BLOCKS, BROWS, 4 * DV)
    image_rows = jnp.zeros_like(blocks_all).at[block_target].set(blocks_all).reshape(SEQ_ROWS, 4 * DV)
    incoming = cotangent.reshape(BLOCKS, BROWS, 4 * DV)[block_target].reshape(PATCHES, DV)
    grad_attn = pull_back(incoming.astype(jnp.float32))[0].astype(jnp.bfloat16)
    grad_out = jnp.dot(head_out.T, grad_attn, preferred_element_type=jnp.float32)
    grad_heads = jnp.dot(grad_attn, out_weight.T, preferred_element_type=jnp.float32).astype(jnp.bfloat16)
    grad_qkv_rows = lax.map(lambda trio: attend_back(trio[0], trio[1], trio[2]), (per_image, patch_counts, grad_heads.reshape(IMAGES, PATCH_MAX, DV)))
    grad_qkv = jnp.dot(normed.T, grad_qkv_rows.reshape(PATCHES, 3 * DV), preferred_element_type=jnp.float32)
    return (image_rows, grad_qkv, grad_out)
```

```python
import functools

import jax
import jax.numpy as jnp
from jax import lax
from jax.experimental import pallas as pl
from jax.experimental.pallas import tpu as pltpu
from jax.sharding import PartitionSpec as P

HEAD_V = 80
NZ = 8
F32 = jnp.float32
BF16 = jnp.bfloat16
I32 = jnp.int32
MESH = pl.DeviceIdType.MESH


def mm(a, b):
    return lax.dot_general(a, b, (((1,), (0,)), ((), ())), preferred_element_type=F32)


def mm_t(a, b):
    return lax.dot_general(a, b, (((1,), (1,)), ((), ())), preferred_element_type=F32)


def iota(shape, dim):
    return lax.broadcasted_iota(I32, shape, dim)


def ones_where(cond):
    return jnp.where(cond, 1.0, 0.0)


def norm_parts(values):
    center = values - jnp.mean(values, axis=-1, keepdims=True)
    spread = jnp.mean(center * center, axis=-1, keepdims=True)
    return center, lax.rsqrt(spread + 1e-06)


def kernel(
    ny,
    nt,
    n_sems,
    counts,
    x_ref,
    ga_ref,
    gm_ref,
    w_ref,
    ow_ref,
    cot_ref,
    bt_ref,
    image_ref,
    gq_ref,
    go_ref,
    wt,
    nrm,
    nrmt,
    qkvt,
    probs,
    ot,
    hs,
    hm,
    wf,
    res,
    bts,
    btz,
    bty,
    btg,
    placing,
    returning,
    cs,
    cyr,
    czr,
    cgr,
    ms,
    myr,
    mzr,
    mgr,
    inc,
    merged,
    gown,
    gownt,
    ghs,
    ghr,
    ght,
    os_,
    ogr,
    oyr,
    ox,
    oxr,
    oz,
    ozr,
    dws,
    dgr,
    dyr,
    dz,
    dzr,
    ssem,
    rsem,
):
    g = lax.axis_index("grp")
    s = lax.axis_index("seq")
    t = lax.axis_index("tp")
    y = lax.div(s, NZ)
    z = lax.rem(s, NZ)
    images = x_ref.shape[0] // 256
    width = x_ref.shape[1]
    heads = w_ref.shape[1] // (3 * HEAD_V)
    hcols = heads * HEAD_V
    half = width // 2
    yrows = half // ny
    zrows = yrows // NZ

    def at_z(k):
        return lax.rem(z + k, NZ)

    def at_y(k):
        return lax.rem(y + k, ny)

    def at_t(k):
        return lax.rem(t + k, nt)

    def dev_z(k):
        return {"seq": y * NZ + at_z(k)}

    def dev_y(k):
        return {"seq": at_y(k) * NZ + z}

    def dev_t(k):
        return {"tp": at_t(k)}

    dev_g = {"grp": 1 - g}

    used = [0]
    copies = {}

    def push(src, dst, device):
        k = used[0]
        used[0] += 1
        copy = pltpu.make_async_remote_copy(
            src_ref=src,
            dst_ref=dst,
            send_sem=ssem.at[k],
            recv_sem=rsem.at[k],
            device_id=device,
            device_id_type=MESH,
        )
        copy.start()
        copies[id(copy)] = copy
        return copy

    def arrived(group):
        for c in group:
            c.wait_recv()

    def sent(group):
        for c in group:
            c.wait_send()
            del copies[id(c)]

    def rows(start, size):
        return pl.ds(pl.multiple_of(start, size if size & (size - 1) == 0 else 16), size)

    barrier = pltpu.get_barrier_semaphore()
    partners = (
        [dev_z(k) for k in range(1, NZ)]
        + [dev_y(k) for k in range(1, ny)]
        + [dev_t(k) for k in range(1, nt)]
        + [dev_g]
    )
    for device in partners:
        pl.semaphore_signal(barrier, inc=1, device_id=device, device_id_type=MESH)

    eye = ones_where(iota((256, 256), 0) == iota((256, 256), 1)).astype(BF16)

    at = 0
    while at < 3 * hcols:
        size = min(256, 3 * hcols - at)
        wt[at : at + size, :] = mm_t(eye[:size, :size], w_ref[:, at : at + size]).astype(BF16)
        at += size

    bt_row = bt_ref[...]
    bts[...] = jnp.broadcast_to(bt_row, bts.shape)
    pl.semaphore_wait(barrier, len(partners))

    slots_z = [push(bts, btz.at[z], dev_z(k)) for k in range(1, NZ)]
    hrows = hcols // 2
    own_half = pl.ds(pl.multiple_of(g * hrows, 16), hrows)
    weight_t = [push(ow_ref.at[own_half, :], wf.at[t, own_half, :], dev_t(k)) for k in range(1, nt)]
    btz[pl.ds(z, 1)] = bts[...][None]
    wf[pl.ds(t, 1)] = ow_ref[...][None]

    gain_a = ga_ref[...]
    gain_m = gm_ref[...]

    def forward_image(i):
        base = i * 256

        def norm_rows(c, _):
            at = pl.ds(pl.multiple_of(c * 32, 32), 32)
            values = x_ref[pl.ds(pl.multiple_of(base + c * 32, 32), 32), :].astype(F32)
            center, scale = norm_parts(values)
            nrm[at, :] = (center * scale * gain_a).astype(BF16)
            return 0

        lax.fori_loop(0, 8, norm_rows, 0)
        own = ones_where(iota((64, 256), 1) == 4 * iota((64, 256), 0) + t).astype(BF16)
        res[base // 4 : base // 4 + 64, :] = mm(own, x_ref[base : base + 256, :])
        for f in range(width // 256):
            nrmt[f * 256 : (f + 1) * 256, base : base + 256] = mm_t(
                eye, nrm[:, f * 256 : (f + 1) * 256]
            ).astype(BF16)

        def project(c, _):
            at = pl.ds(pl.multiple_of(c * 240, 16), 240)
            qkvt[at, base : base + 256] = mm_t(wt[at, :], nrm[...]).astype(BF16)
            return 0

        lax.fori_loop(0, 3 * hcols // 240, project, 0)
        count = counts[i]
        live = iota((256, 128), 0) < count

        def head(h, _):
            row = h * 3 * HEAD_V
            cols = pl.ds(base, 256)
            k_t = qkvt[pl.ds(pl.multiple_of(row + HEAD_V, 16), HEAD_V), cols]
            v_t = qkvt[pl.ds(pl.multiple_of(row + 2 * HEAD_V, 16), HEAD_V), cols]
            k = mm_t(eye, k_t).astype(BF16)
            for c in range(2):
                q_t = qkvt[pl.ds(pl.multiple_of(row, 16), HEAD_V), pl.ds(base + c * 128, 128)]
                scores = mm(k, q_t) * HEAD_V**-0.5
                scores = jnp.where(live, scores, -1e30)
                weights = jnp.exp(scores - jnp.max(scores, axis=0, keepdims=True))
                weights = weights * (1.0 / jnp.sum(weights, axis=0, keepdims=True))
                weights = weights.astype(BF16)
                probs[i * heads + h, :, c * 128 : (c + 1) * 128] = weights
                ot[pl.ds(pl.multiple_of(h * HEAD_V, 16), HEAD_V), c * 128 : (c + 1) * 128] = mm(
                    v_t, weights
                ).astype(BF16)
            return 0

        lax.fori_loop(0, heads, head, 0)
        by_patch = ones_where(
            iota((256, 256), 1) == 4 * (iota((256, 256), 0) & 63) + (iota((256, 256), 0) >> 6)
        ).astype(BF16)
        hs[i] = mm_t(by_patch, ot[...]).astype(BF16)
        out = pl.ds(i * 64, 64)
        made = [
            push(hs.at[i, rows(at_t(k) * 64, 64), :], hm.at[t, out, :], dev_t(k))
            for k in range(1, nt)
        ]
        hm[pl.ds(t, 1), out, :] = hs[i, rows(t * 64, 64), :][None]
        return made

    row_i, lane_i = iota((256, 256), 0), iota((256, 256), 1)

    def y_to_z():
        return ones_where(
            lane_i == ((row_i >> 3) & (ny - 1)) * 64 + (row_i >> 5) * 8 + (row_i & 7)
        ).astype(BF16)

    def z_to_g():
        return ones_where(
            lane_i
            == ((row_i >> 4) & (NZ - 1)) * 32
            + ((row_i >> 2) & (ny - 1)) * 8
            + (row_i >> 7) * 4
            + (row_i & 3)
        ).astype(BF16)

    def g_to_y():
        return ones_where(
            lane_i
            == ((row_i >> 2) & 1) * 128
            + ((row_i >> 3) & (NZ - 1)) * 16
            + (row_i >> 6) * 4
            + (row_i & 3)
        ).astype(BF16)

    def send_y(buf, dst):
        made = [push(buf.at[rows(at_y(k) * 64, 64), :], dst.at[y], dev_y(k)) for k in range(1, ny)]
        dst[pl.ds(y, 1)] = buf[rows(y * 64, 64), :][None]
        return made

    def send_z(buf, dst):
        made = [push(buf.at[rows(at_z(k) * 32, 32), :], dst.at[z], dev_z(k)) for k in range(1, NZ)]
        dst[pl.ds(z, 1)] = buf[rows(z * 32, 32), :][None]
        return made

    def send_g(buf, dst):
        made = [push(buf.at[rows((1 - g) * 128, 128), :], dst.at[g], dev_g)]
        dst[pl.ds(g, 1)] = buf[rows(g * 128, 128), :][None]
        return made

    heads_in = forward_image(0)
    arrived(slots_z)
    slots_y = [push(btz, bty.at[y], dev_y(k)) for k in range(1, ny)]
    bty[pl.ds(y, 1)] = btz[...][None]

    heads_in += forward_image(1)
    arrived(slots_y)
    slots_g = [push(bty, btg.at[g], dev_g)]
    btg[pl.ds(g, 1)] = bty[...][None]

    pair = iota((256, 128), 0)
    block_lane = iota((256, 128), 1)
    target = jnp.broadcast_to(bt_row, (256, 128)).astype(F32)
    target_of = jnp.sum(jnp.where(block_lane == (pair >> 1), target, 0.0), axis=1, keepdims=True)
    target_of = target_of.astype(I32)
    shard_of = target_of >> 7
    earlier = ((jnp.broadcast_to(bt_row, (256, 128)) >> 7) == shard_of) & (block_lane < (pair >> 1))
    rank_of = jnp.sum(ones_where(earlier), axis=1, keepdims=True).astype(I32)
    row_of = iota((256, 1), 0) & 1
    s_g, s_y, s_z = shard_of >> 5, (shard_of >> 3) & (ny - 1), shard_of & (NZ - 1)
    from_at = s_g * 128 + s_z * 16 + s_y * 4 + rank_of * 2 + row_of
    gathering = ones_where(lane_i == from_at).astype(BF16)
    to_at = (s_y * 64 + s_z * 8 + s_g * 4 + rank_of * 2 + row_of).astype(F32)
    to_row = jnp.sum(jnp.where(row_i == lane_i, to_at, 0.0), axis=0, keepdims=True).astype(I32)
    placing[0] = gathering
    placing[1] = ones_where(row_i == to_row).astype(BF16)

    arrived(slots_g)
    lanes3 = (ny * NZ, 8, 128)
    sub3 = iota(lanes3, 1)
    both = jnp.where(sub3 < 4, btg[0].reshape(lanes3), btg[1].reshape(lanes3))
    hit = (both >> 7) == (g * ny * NZ + s)
    slot = (both & 127).astype(F32)
    lane3 = iota(lanes3, 2).astype(F32)
    first_lane = jnp.min(jnp.where(hit, lane3, 999.0), axis=2, keepdims=True)
    first = lane3 == first_lane
    slot_0 = jnp.sum(jnp.where(hit & first, slot, 0.0), axis=2, keepdims=True)
    slot_1 = jnp.sum(jnp.where(hit & (lane3 != first_lane), slot, 0.0), axis=2, keepdims=True)
    sub1 = iota((ny * NZ, 8, 1), 1)
    slot_row = jnp.where((sub1 & 2) == 2, slot_1, slot_0) * 2.0 + (sub1 & 1).astype(F32)
    slot_row = slot_row.reshape(256, 1)
    pick = ones_where(lane_i.astype(F32) == slot_row)
    slot_lane = jnp.sum(jnp.where(row_i == lane_i, slot_row, 0.0), axis=0, keepdims=True)
    returning[...] = ones_where(row_i.astype(F32) == slot_lane).astype(BF16)

    def moved(order, src, dst):
        for f in range(width // 256):
            cols = slice(f * 256, (f + 1) * 256)
            dst[:, cols] = mm(order, src(cols)).astype(BF16)

    moved(pick.astype(BF16), lambda c: cot_ref[:, c], cs)
    cot_y = send_y(cs, cyr)

    heads_in += forward_image(2)
    arrived(weight_t)
    weight_g = []
    for k in range(1, nt):
        piece = wf.at[at_t(nt - k), own_half, :]
        weight_g.append(push(piece, piece, dev_g))
    arrived(cot_y)
    sent(cot_y)
    moved(y_to_z(), lambda c: cyr[:, :, c].reshape(256, 256), cs)
    cot_z = send_z(cs, czr)

    heads_in += forward_image(3)
    arrived(cot_z)
    sent(cot_z)
    moved(z_to_g(), lambda c: czr[:, :, c].reshape(256, 256), cs)
    cot_g = send_g(cs, cgr)
    arrived(heads_in)
    arrived(weight_g)

    def project_out(c, _):
        cols = pl.ds(pl.multiple_of(c * 256, 256), 256)
        total = res[:, cols]
        for q in range(nt):
            total += mm(hm[q], wf[q, :, cols])
        res[:, cols] = total
        return 0

    lax.fori_loop(0, width // 256, project_out, 0)
    arrived(cot_g)
    moved(placing[0], lambda c: cgr[:, :, c].reshape(256, 256), inc)

    def merge_rows(c, _):
        at = pl.ds(pl.multiple_of(c * 32, 32), 32)
        center, scale = norm_parts(res[at, :])
        hat = center * scale
        alive = ones_where(4 * ((iota((32, 1), 0) + c * 32) & 63) < counts[lax.div(c, 2)])
        merged[at, :] = (hat * gain_m * alive).astype(BF16)
        grad = inc[at, :].astype(F32) * alive * gain_m
        mean_grad = jnp.mean(grad, axis=-1, keepdims=True)
        mean_hat = jnp.mean(grad * hat, axis=-1, keepdims=True)
        gown[at, :] = (scale * (grad - mean_grad - hat * mean_hat)).astype(BF16)
        return 0

    lax.fori_loop(0, 8, merge_rows, 0)

    grads_in = []
    for k in (1, 2, 3, 0):
        q = at_t(k)
        ghs[pl.ds(q, 1)] = mm_t(wf[pl.ds(q, 1)].reshape(hcols, width), gown[...]).astype(BF16)[None]
        if k:
            grads_in.append(push(ghs.at[q], ghr.at[t], dev_t(k)))
        else:
            ghr[pl.ds(q, 1)] = ghs[pl.ds(q, 1)]

    moved(placing[1], lambda c: merged[:, c], ms)
    row_y = send_y(ms, myr)

    for f in range(width // 256):
        gownt[f * 256 : (f + 1) * 256, :] = mm_t(eye, gown[:, f * 256 : (f + 1) * 256]).astype(BF16)

    their_rows = pl.ds(pl.multiple_of((1 - g) * half, 128), half)
    own_rows = pl.ds(pl.multiple_of(g * half, 128), half)

    def out_terms(side):
        def one(q, _):
            for c in range(2):
                at = pl.ds(pl.multiple_of(side * half + c * (half // 2), 64), half // 2)
                os_[q, at, :] = mm(gownt[at, :], hm[q]).astype(BF16)
            return 0

        lax.fori_loop(0, nt, one, 0)

    out_terms(1 - g)
    out_g = [push(os_.at[:, their_rows, :], ogr, dev_g)]
    out_terms(g)

    arrived(grads_in)

    def spread(i, _):
        cols = pl.ds(pl.multiple_of(i * 256, 256), 256)
        total = jnp.zeros((hcols, 256), F32)
        for p in range(nt):
            order = ones_where(lane_i == 4 * (row_i - 64 * i) + p).astype(BF16)
            total += mm(ghr[p], order)
        ght[:, cols] = total.astype(BF16)
        return 0

    lax.fori_loop(0, images, spread, 0)

    def back_head(h):
        row = h * 3 * HEAD_V

        def back_image(i, _):
            cols = pl.ds(pl.multiple_of(i * 256, 256), 256)
            at_q, at_k, at_v = row, row + HEAD_V, row + 2 * HEAD_V
            q_t = qkvt[at_q : at_q + HEAD_V, cols]
            k_t = qkvt[at_k : at_k + HEAD_V, cols]
            v_t = qkvt[at_v : at_v + HEAD_V, cols]
            d_t = ght[h * HEAD_V : (h + 1) * HEAD_V, cols]
            v = mm_t(eye, v_t).astype(BF16)
            weights = probs[i * heads + h]
            grad_v = mm_t(d_t, weights).astype(BF16)
            parts = []
            for c in range(2):
                lanes = slice(c * 128, (c + 1) * 128)
                w = weights[:, lanes].astype(F32)
                grad_w = mm(v, d_t[:, lanes]).astype(BF16).astype(F32)
                inner = jnp.sum(w * grad_w, axis=0, keepdims=True)
                parts.append((w * (grad_w - inner) * HEAD_V**-0.5).astype(BF16))
            grad_s = jnp.concatenate(parts, axis=1)
            grad_q = mm(k_t, grad_s).astype(BF16)
            grad_k = mm_t(q_t, grad_s).astype(BF16)
            qkvt[at_q : at_q + HEAD_V, cols] = grad_q
            qkvt[at_k : at_k + HEAD_V, cols] = grad_k
            qkvt[at_v : at_v + HEAD_V, cols] = grad_v
            return 0

        lax.fori_loop(0, images, back_image, 0)

    def weight_terms(h, side):
        def one(c, _):
            at = pl.ds(pl.multiple_of(side * half + c * (half // 2), 64), half // 2)
            dws[h, at, :] = mm_t(
                nrmt[at, :], qkvt[h * 3 * HEAD_V : (h + 1) * 3 * HEAD_V, :]
            ).astype(BF16)
            return 0

        lax.fori_loop(0, 2, one, 0)

    def to_shards():
        r, c = iota((NZ * 32, yrows), 0), iota((NZ * 32, yrows), 1)
        return ones_where((c == (r >> 5) * zrows + (r & 31)) & ((r & 31) < zrows)).astype(BF16)

    def add(a, b):
        return a.astype(F32) + b.astype(F32)

    def weight_start(h):
        weight_terms(h, 1 - g)
        made = [push(dws.at[h, their_rows, :], dgr.at[h], dev_g)]
        weight_terms(h, g)
        return made

    def weight_y(h, group):
        arrived(group)
        dws[h, own_rows, :] = add(dws[h, own_rows, :], dgr[h]).astype(BF16)
        return [
            push(
                dws.at[h, pl.ds(pl.multiple_of(g * half + at_y(k) * yrows, 16), yrows), :],
                dyr.at[h, k - 1],
                dev_y(k),
            )
            for k in range(1, ny)
        ]

    def weight_z(h, group):
        arrived(group)
        total = dws[h, pl.ds(pl.multiple_of(g * half + y * yrows, 16), yrows), :].astype(F32)
        for k in range(1, ny):
            total += dyr[h, k - 1].astype(F32)
        dz[h] = mm(to_shards(), total.astype(BF16)).astype(BF16)
        return [
            push(dz.at[h, rows(at_z(k) * 32, 32), :], dzr.at[h, k - 1], dev_z(k))
            for k in range(1, NZ)
        ]

    def weight_end(h, group):
        arrived(group)
        total = dz[h, rows(z * 32, 32), :].astype(F32)
        for k in range(1, NZ):
            total += dzr[h, k - 1].astype(F32)
        gq_ref[h] = total

    def out_y(group):
        arrived(group)
        for q in range(nt):
            os_[q, own_rows, :] = add(os_[q, own_rows, :], ogr[q]).astype(BF16)
        return [
            push(
                os_.at[:, pl.ds(pl.multiple_of(g * half + at_y(k) * yrows, 16), yrows), :],
                oyr.at[k - 1],
                dev_y(k),
            )
            for k in range(1, ny)
        ]

    def out_x(group):
        arrived(group)
        mine = pl.ds(pl.multiple_of(g * half + y * yrows, 16), yrows)
        for q in range(nt):
            total = os_[q, mine, :].astype(F32)
            for k in range(1, ny):
                total += oyr[k - 1, q].astype(F32)
            ox[q] = total.astype(BF16)
        return [push(ox.at[at_t(k)], oxr.at[k - 1], dev_t(k)) for k in range(1, nt)]

    def out_z(group):
        arrived(group)
        total = ox[pl.ds(t, 1)].reshape(yrows, hcols).astype(F32)
        for k in range(1, nt):
            total += oxr[k - 1].astype(F32)
        oz[...] = mm(to_shards(), total.astype(BF16)).astype(BF16)
        return [
            push(oz.at[rows(at_z(k) * 32, 32), :], ozr.at[k - 1], dev_z(k)) for k in range(1, NZ)
        ]

    def out_end(group):
        arrived(group)
        total = oz[rows(z * 32, 32), :].astype(F32)
        for k in range(1, NZ):
            total += ozr[k - 1].astype(F32)
        go_ref[...] = total

    back_head(0)
    w0 = weight_start(0)
    o = out_y(out_g)
    arrived(row_y)
    sent(row_y)
    moved(y_to_z(), lambda c: myr[:, :, c].reshape(256, 256), ms)
    row_z = send_z(ms, mzr)

    back_head(1)
    w0 = weight_y(0, w0)
    w1 = weight_start(1)
    o = out_x(o)

    back_head(2)
    w0 = weight_z(0, w0)
    w1 = weight_y(1, w1)
    w2 = weight_start(2)
    o = out_z(o)
    arrived(row_z)
    sent(row_z)
    moved(z_to_g(), lambda c: mzr[:, :, c].reshape(256, 256), ms)
    row_g = send_g(ms, mgr)

    back_head(3)
    w2 = weight_y(2, w2)
    w3 = weight_start(3)
    w1 = weight_z(1, w1)
    weight_end(0, w0)
    w3 = weight_y(3, w3)
    w2 = weight_z(2, w2)
    out_end(o)
    arrived(row_g)
    moved(g_to_y(), lambda c: mgr[:, :, c].reshape(256, 256), inc)
    moved(returning[...], lambda c: inc[:, c], image_ref)
    weight_end(1, w1)
    w3 = weight_z(3, w3)
    weight_end(2, w2)
    weight_end(3, w3)
    for c in copies.values():
        c.wait_send()
    assert used[0] == n_sems


def shards(
    ny, nt, patches_in, gain_attn, gain_merge, qkv_weight, out_weight, cotangent, patch_counts, block_target
):
    row_count, width = patches_in.shape
    images = patch_counts.shape[0]
    hcols = out_weight.shape[0]
    heads = hcols // HEAD_V
    cols = 3 * HEAD_V
    half, yrows = width // 2, width // 2 // ny
    n_sems = (
        (NZ - 1 + ny - 1 + 1)
        + 2 * (nt - 1)
        + images * (nt - 1)
        + 2 * (NZ - 1 + ny - 1 + 1)
        + (nt - 1)
        + (1 + ny - 1 + nt - 1 + NZ - 1)
        + heads * (1 + ny - 1 + NZ - 1)
    )
    v = pltpu.VMEM
    scratch = [
        v((3 * hcols, width), BF16),
        v((256, width), BF16),
        v((width, row_count), BF16),
        v((3 * hcols, row_count), BF16),
        v((images * heads, 256, 256), BF16),
        v((hcols, 256), BF16),
        v((images, 256, hcols), BF16),
        v((nt, 256, hcols), BF16),
        v((nt, hcols, width), BF16),
        v((256, width), F32),
        v((8, 128), I32),
        v((NZ, 8, 128), I32),
        v((ny, NZ, 8, 128), I32),
        v((2, ny, NZ, 8, 128), I32),
        v((2, 256, 256), BF16),
        v((256, 256), BF16),
        v((256, width), BF16),
        v((ny, 64, width), BF16),
        v((NZ, 32, width), BF16),
        v((2, 128, width), BF16),
        v((256, width), BF16),
        v((ny, 64, width), BF16),
        v((NZ, 32, width), BF16),
        v((2, 128, width), BF16),
        v((256, width), BF16),
        v((256, width), BF16),
        v((256, width), BF16),
        v((width, 256), BF16),
        v((nt, hcols, 256), BF16),
        v((nt, hcols, 256), BF16),
        v((hcols, row_count), BF16),
        v((nt, width, hcols), BF16),
        v((nt, half, hcols), BF16),
        v((ny - 1, nt, yrows, hcols), BF16),
        v((nt, yrows, hcols), BF16),
        v((nt - 1, yrows, hcols), BF16),
        v((NZ * 32, hcols), BF16),
        v((NZ - 1, 32, hcols), BF16),
        v((heads, width, cols), BF16),
        v((heads, half, cols), BF16),
        v((heads, ny - 1, yrows, cols), BF16),
        v((heads, NZ * 32, cols), BF16),
        v((heads, NZ - 1, 32, cols), BF16),
        pltpu.SemaphoreType.DMA((n_sems,)),
        pltpu.SemaphoreType.DMA((n_sems,)),
    ]
    in_vmem = pl.BlockSpec(memory_space=pltpu.VMEM)
    image_rows, gq, go = pl.pallas_call(
        functools.partial(kernel, ny, nt, n_sems),
        out_shape=(
            jax.ShapeDtypeStruct((256, width), BF16),
            jax.ShapeDtypeStruct((heads, 32, cols), F32),
            jax.ShapeDtypeStruct((32, hcols), F32),
        ),
        in_specs=[pl.BlockSpec(memory_space=pltpu.SMEM)] + [in_vmem] * 7,
        out_specs=(in_vmem,) * 3,
        scratch_shapes=scratch,
        compiler_params=pltpu.CompilerParams(
            collective_id=0, has_side_effects=True, vmem_limit_bytes=62 << 20
        ),
        name="block",
    )(
        patch_counts,
        patches_in,
        gain_attn.reshape(1, width),
        gain_merge.reshape(1, width),
        qkv_weight,
        out_weight,
        cotangent,
        block_target.reshape(1, -1),
    )
    zrows = yrows // NZ
    grad_qkv = jnp.moveaxis(gq[:, :zrows], 0, 1).reshape(zrows, heads * cols)
    grad_out = go[:zrows].T
    return image_rows, grad_qkv, grad_out


def solution(mesh):
    ny, nt = mesh.shape["seq"] // NZ, mesh.shape["tp"]
    return jax.shard_map(
        functools.partial(shards, ny, nt),
        mesh=mesh,
        in_specs=(
            P(("grp", "seq"), None),
            P(),
            P(),
            P(None, "tp"),
            P("tp", None),
            P(("grp", "seq"), "tp"),
            P(("grp", "seq")),
            P(("grp", "seq")),
        ),
        out_specs=(P(("grp", "seq"), "tp"), P(("grp", "seq"), "tp"), P("tp", ("grp", "seq"))),
        check_vma=False,
    )
```

```python
import functools

import jax
import jax.numpy as jnp
from jax import lax
from jax.experimental import pallas as pl
from jax.experimental.pallas import tpu as pltpu
from jax.sharding import PartitionSpec as P

HEAD_V = 80
NZ = 8
F32 = jnp.float32
BF16 = jnp.bfloat16
I32 = jnp.int32
MESH = pl.DeviceIdType.MESH


def mm(a, b):
    return lax.dot_general(a, b, (((1,), (0,)), ((), ())), preferred_element_type=F32)


def mm_t(a, b):
    return lax.dot_general(a, b, (((1,), (1,)), ((), ())), preferred_element_type=F32)


def iota(shape, dim):
    return lax.broadcasted_iota(I32, shape, dim)


def ones_where(cond):
    return jnp.where(cond, 1.0, 0.0)


def norm_parts(values):
    center = values - jnp.mean(values, axis=-1, keepdims=True)
    spread = jnp.mean(center * center, axis=-1, keepdims=True)
    return center, lax.rsqrt(spread + 1e-06)


def kernel(
    ny,
    nt,
    n_sems,
    counts,
    ga_ref,
    gm_ref,
    bt_ref,
    x_hbm,
    wt_hbm,
    ow_hbm,
    cot_hbm,
    image_ref,
    gq_ref,
    go_ref,
    x_ref,
    wt,
    cot_ref,
    nrm,
    nrmt,
    qkvt,
    probs,
    ot,
    hs,
    hm,
    wf,
    res,
    bts,
    bty,
    btz,
    btg,
    placing,
    returning,
    cs,
    cyr,
    czr,
    cgr,
    ms,
    myr,
    mzr,
    mgr,
    inc,
    merged,
    gown,
    gownt,
    hmt,
    ghs,
    ghr,
    ght,
    oa,
    oag,
    oax,
    oay,
    oayr,
    oaz,
    oazr,
    ob,
    obg,
    obyr,
    obx,
    obxr,
    obz,
    obzr,
    dws,
    dgr,
    dyr,
    dz,
    dzr,
    lsem,
    ssem,
    rsem,
):
    g = lax.axis_index("grp")
    s = lax.axis_index("seq")
    t = lax.axis_index("tp")
    y = lax.div(s, NZ)
    z = lax.rem(s, NZ)
    images = x_ref.shape[0] // 256
    width = x_ref.shape[1]
    hcols = wt.shape[0] // 3
    heads = hcols // HEAD_V
    half = width // 2
    yrows = half // ny
    zrows = yrows // NZ

    def at_z(k):
        return lax.rem(z + k, NZ)

    def at_y(k):
        return lax.rem(y + k, ny)

    def at_t(k):
        return lax.rem(t + k, nt)

    def dev_z(k):
        return {"seq": y * NZ + at_z(k)}

    def dev_y(k):
        return {"seq": at_y(k) * NZ + z}

    def dev_t(k):
        return {"tp": at_t(k)}

    dev_g = {"grp": 1 - g}
    to_t = (1, 3, 2)

    used = [0]
    copies = {}

    def push(src, dst, device):
        k = used[0]
        used[0] += 1
        copy = pltpu.make_async_remote_copy(
            src_ref=src,
            dst_ref=dst,
            send_sem=ssem.at[k],
            recv_sem=rsem.at[k],
            device_id=device,
            device_id_type=MESH,
        )
        copy.start()
        copies[id(copy)] = copy
        return copy

    def arrived(group):
        for c in group:
            c.wait_recv()

    def sent(group):
        for c in group:
            c.wait_send()
            del copies[id(c)]

    def rows(start, size):
        return pl.ds(pl.multiple_of(start, size if size & (size - 1) == 0 else 16), size)

    barrier = pltpu.get_barrier_semaphore()
    partners = (
        [dev_z(k) for k in range(1, NZ)]
        + [dev_y(k) for k in range(1, ny)]
        + [dev_t(k) for k in range(1, nt)]
        + [dev_g]
    )
    for device in partners:
        pl.semaphore_signal(barrier, inc=1, device_id=device, device_id_type=MESH)

    def image_rows_of(i):
        at = pl.ds(i * 256, 256)
        return pltpu.make_async_copy(x_hbm.at[at, :], x_ref.at[at, :], lsem.at[i])

    loads_x = [image_rows_of(i) for i in range(images)]
    load_w = pltpu.make_async_copy(wt_hbm, wt, lsem.at[images])
    load_c = pltpu.make_async_copy(cot_hbm, cot_ref, lsem.at[images + 1])
    load_o = pltpu.make_async_copy(ow_hbm, wf.at[t], lsem.at[images + 2])
    loads_x[0].start()
    load_w.start()
    load_c.start()

    eye = ones_where(iota((256, 256), 0) == iota((256, 256), 1)).astype(BF16)
    bt_row = bt_ref[...]
    bts[...] = jnp.broadcast_to(bt_row, bts.shape)
    pl.semaphore_wait(barrier, len(partners))

    slots_y = [push(bts, bty.at[y], dev_y(k)) for k in range(1, ny)]
    hrows = hcols // 2
    own_half = pl.ds(pl.multiple_of(g * hrows, 16), hrows)
    weight_t = [
        push(ow_hbm.at[own_half, :], wf.at[t, own_half, :], dev_t(k)) for k in range(1, nt)
    ]
    for load in loads_x[1:]:
        load.start()
    load_o.start()
    bty[pl.ds(y, 1)] = bts[...][None]

    gain_a = ga_ref[...].reshape(1, width)
    gain_m = gm_ref[...].reshape(1, width)

    def forward_norm(i):
        base = i * 256
        loads_x[i].wait()

        def norm_rows(c, _):
            at = pl.ds(pl.multiple_of(c * 32, 32), 32)
            values = x_ref[pl.ds(pl.multiple_of(base + c * 32, 32), 32), :].astype(F32)
            center, scale = norm_parts(values)
            nrm[at, :] = (center * scale * gain_a).astype(BF16)
            return 0

        lax.fori_loop(0, 8, norm_rows, 0)
        own = ones_where(iota((64, 256), 1) == 4 * iota((64, 256), 0) + t).astype(BF16)
        res[base // 4 : base // 4 + 64, :] = mm(own, x_ref[base : base + 256, :])
        for f in range(width // 256):
            nrmt[f * 256 : (f + 1) * 256, base : base + 256] = mm_t(
                eye, nrm[:, f * 256 : (f + 1) * 256]
            ).astype(BF16)

    def forward_qkv(i):
        base = i * 256
        if i == 0:
            load_w.wait()

        def project(c, _):
            at = pl.ds(pl.multiple_of(c * 240, 16), 240)
            qkvt[at, base : base + 256] = mm_t(wt[at, :], nrm[...]).astype(BF16)
            return 0

        lax.fori_loop(0, 3 * hcols // 240, project, 0)

    def forward_attend(i):
        base = i * 256
        live = iota((256, 128), 0) < counts[i]
        cols = pl.ds(base, 256)
        for h in range(heads):
            row = h * 3 * HEAD_V
            k = mm_t(eye, qkvt[row + HEAD_V : row + 2 * HEAD_V, cols]).astype(BF16)
            v_t = qkvt[row + 2 * HEAD_V : row + 3 * HEAD_V, cols]
            for c in range(2):
                lanes = slice(c * 128, (c + 1) * 128)
                q_t = qkvt[row : row + HEAD_V, pl.ds(base + c * 128, 128)]
                scores = mm(k, q_t) * HEAD_V**-0.5
                scores = jnp.where(live, scores, -1e30)
                weights = jnp.exp(scores - jnp.max(scores, axis=0, keepdims=True))
                weights = weights * (1.0 / jnp.sum(weights, axis=0, keepdims=True))
                weights = weights.astype(BF16)
                probs[i * heads + h, :, lanes] = weights
                ot[h * HEAD_V : (h + 1) * HEAD_V, lanes] = mm(v_t, weights).astype(BF16)
        by_patch = ones_where(
            iota((256, 256), 1) == 4 * (iota((256, 256), 0) & 63) + (iota((256, 256), 0) >> 6)
        ).astype(BF16)
        hs[i] = mm_t(by_patch, ot[...]).astype(BF16)
        out = pl.ds(i * 64, 64)
        made = [
            push(hs.at[i, rows(at_t(k) * 64, 64), :], hm.at[t, out, :], dev_t(k)) for k in to_t
        ]
        hm[pl.ds(t, 1), out, :] = hs[i, rows(t * 64, 64), :][None]
        return made

    row_i, lane_i = iota((256, 256), 0), iota((256, 256), 1)

    def z_to_y():
        return ones_where(
            lane_i == ((row_i >> 3) & (NZ - 1)) * 32 + (row_i >> 6) * 8 + (row_i & 7)
        ).astype(BF16)

    def y_to_g():
        return ones_where(
            lane_i
            == ((row_i >> 5) & (ny - 1)) * 64
            + ((row_i >> 2) & (NZ - 1)) * 8
            + (row_i >> 7) * 4
            + (row_i & 3)
        ).astype(BF16)

    def g_to_z():
        return ones_where(
            lane_i
            == ((row_i >> 2) & 1) * 128
            + ((row_i >> 3) & (ny - 1)) * 32
            + (row_i >> 5) * 4
            + (row_i & 3)
        ).astype(BF16)

    def send_y(buf, dst):
        made = [push(buf.at[rows(at_y(k) * 64, 64), :], dst.at[y], dev_y(k)) for k in (1, 3, 2)]
        dst[pl.ds(y, 1)] = buf[rows(y * 64, 64), :][None]
        return made

    def send_z(buf, dst):
        made = [
            push(buf.at[rows(at_z(k) * 32, 32), :], dst.at[z], dev_z(k))
            for k in (4, 3, 5, 2, 6, 1, 7)
        ]
        dst[pl.ds(z, 1)] = buf[rows(z * 32, 32), :][None]
        return made

    def send_g(buf, dst):
        made = [push(buf.at[rows((1 - g) * 128, 128), :], dst.at[g], dev_g)]
        dst[pl.ds(g, 1)] = buf[rows(g * 128, 128), :][None]
        return made

    def moved(order, src, dst):
        for f in range(width // 256):
            cols = slice(f * 256, (f + 1) * 256)
            dst[:, cols] = mm(order, src(cols)).astype(BF16)

    forward_norm(0)
    arrived(slots_y)
    slots_z = [push(bty, btz.at[z], dev_z(k)) for k in range(1, NZ)]
    btz[pl.ds(z, 1)] = bty[...][None]
    forward_qkv(0)
    arrived(slots_z)
    slots_g = [push(btz, btg.at[g], dev_g)]
    btg[pl.ds(g, 1)] = btz[...][None]

    pair = iota((256, 128), 0)
    block_lane = iota((256, 128), 1)
    target = jnp.broadcast_to(bt_row, (256, 128)).astype(F32)
    target_of = jnp.sum(jnp.where(block_lane == (pair >> 1), target, 0.0), axis=1, keepdims=True)
    target_of = target_of.astype(I32)
    shard_of = target_of >> 7
    earlier = ((jnp.broadcast_to(bt_row, (256, 128)) >> 7) == shard_of) & (block_lane < (pair >> 1))
    rank_of = jnp.sum(ones_where(earlier), axis=1, keepdims=True).astype(I32)
    row_of = rank_of * 2 + (iota((256, 1), 0) & 1)
    s_g, s_y, s_z = shard_of >> 5, (shard_of >> 3) & (ny - 1), shard_of & (NZ - 1)
    placing[0] = ones_where(lane_i == shard_of * 4 + row_of).astype(BF16)
    to_at = (s_z * 32 + s_y * 8 + s_g * 4 + row_of).astype(F32)
    to_row = jnp.sum(jnp.where(row_i == lane_i, to_at, 0.0), axis=0, keepdims=True).astype(I32)
    placing[1] = ones_where(row_i == to_row).astype(BF16)

    arrived(slots_g)
    lanes3 = (ny * NZ, 8, 128)
    sub3 = iota(lanes3, 1)
    both = jnp.where(sub3 < 4, btg[0].reshape(lanes3), btg[1].reshape(lanes3))
    hit = (both >> 7) == (g * ny * NZ + s)
    slot = (both & 127).astype(F32)
    lane3 = iota(lanes3, 2).astype(F32)
    first_lane = jnp.min(jnp.where(hit, lane3, 999.0), axis=2, keepdims=True)
    slot_0 = jnp.sum(jnp.where(hit & (lane3 == first_lane), slot, 0.0), axis=2, keepdims=True)
    slot_1 = jnp.sum(jnp.where(hit & (lane3 != first_lane), slot, 0.0), axis=2, keepdims=True)
    sub1 = iota((ny * NZ, 8, 1), 1)
    slot_row = jnp.where((sub1 & 2) == 2, slot_1, slot_0) * 2.0 + (sub1 & 1).astype(F32)
    slot_row = slot_row.reshape(256, 1)
    pick = ones_where(lane_i.astype(F32) == slot_row).astype(BF16)
    load_c.wait()
    moved(pick, lambda c: cot_ref[:, c], cs)
    cot_z = send_z(cs, czr)

    heads_in = forward_attend(0)
    slot_lane = jnp.sum(jnp.where(row_i == lane_i, slot_row, 0.0), axis=0, keepdims=True)
    back_at = ones_where(row_i.astype(F32) == slot_lane).astype(BF16)
    returning[...] = mm(back_at, g_to_z()).astype(BF16)

    forward_norm(1)
    forward_qkv(1)
    heads_in += forward_attend(1)
    forward_norm(2)
    forward_qkv(2)
    heads_in += forward_attend(2)
    arrived(cot_z)
    sent(cot_z)
    moved(z_to_y(), lambda c: czr[:, :, c].reshape(256, 256), cs)
    cot_y = send_y(cs, cyr)
    arrived(weight_t)
    weight_g = []
    for k in range(1, nt):
        piece = wf.at[at_t(nt - k), own_half, :]
        weight_g.append(push(piece, piece, dev_g))
    forward_norm(3)
    forward_qkv(3)
    heads_in += forward_attend(3)
    arrived(cot_y)
    sent(cot_y)
    moved(y_to_g(), lambda c: cyr[:, :, c].reshape(256, 256), cs)
    cot_g = send_g(cs, cgr)
    load_o.wait()
    arrived(heads_in)
    arrived(weight_g)

    def project_out(c, _):
        cols = pl.ds(pl.multiple_of(c * 256, 256), 256)
        total = res[:, cols]
        for q in range(nt):
            total += mm(hm[q], wf[q, :, cols])
        res[:, cols] = total
        return 0

    lax.fori_loop(0, width // 256, project_out, 0)
    arrived(cot_g)
    moved(placing[0], lambda c: cgr[:, :, c].reshape(256, 256), inc)

    def merge_rows(c, _):
        at = pl.ds(pl.multiple_of(c * 32, 32), 32)
        center, scale = norm_parts(res[at, :])
        hat = center * scale
        alive = ones_where(4 * ((iota((32, 1), 0) + c * 32) & 63) < counts[lax.div(c, 2)])
        merged[at, :] = (hat * gain_m * alive).astype(BF16)
        grad = inc[at, :].astype(F32) * alive * gain_m
        mean_grad = jnp.mean(grad, axis=-1, keepdims=True)
        mean_hat = jnp.mean(grad * hat, axis=-1, keepdims=True)
        gown[at, :] = (scale * (grad - mean_grad - hat * mean_hat)).astype(BF16)
        return 0

    lax.fori_loop(0, 8, merge_rows, 0)

    pairs = 2
    prows = hcols // pairs
    for k in to_t + (0,):
        q = at_t(k)
        ghs[pl.ds(q, 1)] = mm_t(wf[pl.ds(q, 1)].reshape(hcols, width), gown[...]).astype(BF16)[None]
    grads_in = [
        [
            push(
                ghs.at[at_t(k), pl.ds(j * prows, prows), :],
                ghr.at[t, pl.ds(j * prows, prows), :],
                dev_t(k),
            )
            for k in to_t
        ]
        for j in range(pairs)
    ]
    ghr[pl.ds(t, 1)] = ghs[pl.ds(t, 1)]

    moved(placing[1], lambda c: merged[:, c], ms)
    row_z = send_z(ms, mzr)

    for f in range(width // 256):
        gownt[f * 256 : (f + 1) * 256, :] = mm_t(eye, gown[:, f * 256 : (f + 1) * 256]).astype(BF16)
    wide = hcols - 128
    for q in range(nt):
        hmt[q] = mm_t(eye[:wide, :wide], hm[q, :, 128:]).astype(BF16)

    def terms_b(side):
        def one(c, _):
            at = pl.ds(pl.multiple_of(side * half + c * (half // 2), 64), half // 2)
            to = pl.ds(pl.multiple_of(c * (half // 2), 64), half // 2)
            for q in range(nt):
                ob[pl.ds(side, 1), to, q * 128 : (q + 1) * 128] = mm(
                    gownt[at, :], hm[q, :, :128]
                ).astype(BF16)[None]
            return 0

        lax.fori_loop(0, 2, one, 0)

    def terms_a(side, k):
        cols = pl.ds(pl.multiple_of(side * half, 128), half)
        q = at_t(k)
        value = mm(hmt[pl.ds(q, 1)].reshape(wide, 256), gown[:, cols])
        oa[pl.ds(side, 1), pl.ds(q, 1)] = value.astype(BF16)[None, None]

    terms_b(1 - g)
    b_g = [push(ob.at[1 - g], obg, dev_g)]
    a_g = []
    for k in to_t + (0,):
        terms_a(1 - g, k)
        a_g.append([push(oa.at[1 - g, at_t(k)], oag.at[at_t(k)], dev_g)])
    terms_b(g)
    for k in to_t + (0,):
        terms_a(g, k)

    def spread(j):
        def one(i, _):
            cols = pl.ds(pl.multiple_of(i * 256, 256), 256)
            total = jnp.zeros((prows, 256), F32)
            for p in range(nt):
                order = ones_where(lane_i == 4 * (row_i - 64 * i) + p).astype(BF16)
                total += mm(ghr[p, j * prows : (j + 1) * prows, :], order)
            ght[j * prows : (j + 1) * prows, cols] = total.astype(BF16)
            return 0

        lax.fori_loop(0, images, one, 0)

    def back_head(h):
        row = h * 3 * HEAD_V

        def back_image(i, _):
            cols = pl.ds(pl.multiple_of(i * 256, 256), 256)
            at_q, at_k, at_v = row, row + HEAD_V, row + 2 * HEAD_V
            q_t = qkvt[at_q : at_q + HEAD_V, cols]
            k_t = qkvt[at_k : at_k + HEAD_V, cols]
            v_t = qkvt[at_v : at_v + HEAD_V, cols]
            d_t = ght[h * HEAD_V : (h + 1) * HEAD_V, cols]
            v = mm_t(eye, v_t).astype(BF16)
            weights = probs[i * heads + h]
            grad_v = mm_t(d_t, weights).astype(BF16)
            parts = []
            for c in range(2):
                lanes = slice(c * 128, (c + 1) * 128)
                w = weights[:, lanes].astype(F32)
                grad_w = mm(v, d_t[:, lanes]).astype(BF16).astype(F32)
                inner = jnp.sum(w * grad_w, axis=0, keepdims=True)
                parts.append((w * (grad_w - inner) * HEAD_V**-0.5).astype(BF16))
            grad_s = jnp.concatenate(parts, axis=1)
            grad_q = mm(k_t, grad_s).astype(BF16)
            grad_k = mm_t(q_t, grad_s).astype(BF16)
            qkvt[at_q : at_q + HEAD_V, cols] = grad_q
            qkvt[at_k : at_k + HEAD_V, cols] = grad_k
            qkvt[at_v : at_v + HEAD_V, cols] = grad_v
            return 0

        lax.fori_loop(0, images, back_image, 0)

    def weight_terms(h, side):
        def one(c, _):
            at = pl.ds(pl.multiple_of(side * half + c * (half // 2), 64), half // 2)
            dws[h, at, :] = mm_t(
                nrmt[at, :], qkvt[h * 3 * HEAD_V : (h + 1) * 3 * HEAD_V, :]
            ).astype(BF16)
            return 0

        lax.fori_loop(0, 2, one, 0)

    def to_shards():
        r, c = iota((NZ * 32, yrows), 0), iota((NZ * 32, yrows), 1)
        return ones_where((c == (r >> 5) * zrows + (r & 31)) & ((r & 31) < zrows)).astype(BF16)

    def add(a, b):
        return a.astype(F32) + b.astype(F32)

    their_rows = pl.ds(pl.multiple_of((1 - g) * half, 128), half)
    own_rows = pl.ds(pl.multiple_of(g * half, 128), half)
    order_y = [(k, k - 1) for k in (1, 3, 2)]
    order_z = [(k, k - 1) for k in (4, 3, 5, 2, 6, 1, 7)]

    def rows_y(k):
        return pl.ds(pl.multiple_of(at_y(k) * yrows, 16), yrows)

    def weight_start(h):
        weight_terms(h, 1 - g)
        made = [push(dws.at[h, their_rows, :], dgr.at[h], dev_g)]
        weight_terms(h, g)
        return made

    def weight_y(h, group):
        arrived(group)
        dgr[h] = add(dws[h, own_rows, :], dgr[h]).astype(BF16)
        return [push(dgr.at[h, rows_y(k), :], dyr.at[h, j], dev_y(k)) for k, j in order_y]

    def weight_z(h, group):
        arrived(group)
        total = dgr[h, rows_y(0), :].astype(F32)
        for k in range(1, ny):
            total += dyr[h, k - 1].astype(F32)
        dz[h] = mm(to_shards(), total.astype(BF16)).astype(BF16)
        return [
            push(dz.at[h, rows(at_z(k) * 32, 32), :], dzr.at[h, j], dev_z(k)) for k, j in order_z
        ]

    def weight_end(h, group):
        arrived(group)
        total = dz[h, rows(z * 32, 32), :].astype(F32)
        for k in range(1, NZ):
            total += dzr[h, k - 1].astype(F32)
        gq_ref[h] = total

    def b_y(group):
        arrived(group)
        obg[...] = add(ob[pl.ds(g, 1)].reshape(half, nt * 128), obg[...]).astype(BF16)
        return [push(obg.at[rows_y(k), :], obyr.at[j], dev_y(k)) for k, j in order_y]

    def b_x(group):
        arrived(group)
        total = obg[rows_y(0), :].astype(F32)
        for k in range(1, ny):
            total += obyr[k - 1].astype(F32)
        for q in range(nt):
            obx[q] = total[:, q * 128 : (q + 1) * 128].astype(BF16)
        return [push(obx.at[at_t(k)], obxr.at[k - 1], dev_t(k)) for k in to_t]

    def b_z(group):
        arrived(group)
        total = obx[pl.ds(t, 1)].reshape(yrows, 128).astype(F32)
        for k in range(1, nt):
            total += obxr[k - 1].astype(F32)
        obz[...] = mm(to_shards(), total.astype(BF16)).astype(BF16)
        return [push(obz.at[rows(at_z(k) * 32, 32), :], obzr.at[j], dev_z(k)) for k, j in order_z]

    def b_end(group):
        arrived(group)
        total = obz[rows(z * 32, 32), :].astype(F32)
        for k in range(1, NZ):
            total += obzr[k - 1].astype(F32)
        go_ref[:, :128] = total

    def a_x(groups):
        made = []
        for k, group in zip(to_t + (0,), groups):
            arrived(group)
            q = at_t(k)
            mine = oa[pl.ds(g, 1), pl.ds(q, 1)].reshape(wide, half)
            oag[pl.ds(q, 1)] = add(mine, oag[pl.ds(q, 1)].reshape(wide, half)).astype(BF16)[None]
            if k:
                made.append(push(oag.at[q], oax.at[k - 1], dev_t(k)))
        return made

    def a_y(group):
        arrived(group)
        for f in range(half // 128):
            cols = slice(f * 128, (f + 1) * 128)
            total = oag[pl.ds(t, 1), :, cols].reshape(wide, 128).astype(F32)
            for k in range(1, nt):
                total += oax[k - 1, :, cols].astype(F32)
            oay[cols, :] = mm_t(eye[:128, :128], total.astype(BF16)).astype(BF16)
        return [push(oay.at[rows_y(k), :], oayr.at[j], dev_y(k)) for k, j in order_y]

    def a_z(group):
        arrived(group)
        total = oay[rows_y(0), :].astype(F32)
        for k in range(1, ny):
            total += oayr[k - 1].astype(F32)
        oaz[...] = mm(to_shards(), total.astype(BF16)).astype(BF16)
        return [push(oaz.at[rows(at_z(k) * 32, 32), :], oazr.at[j], dev_z(k)) for k, j in order_z]

    def a_end(group):
        arrived(group)
        total = oaz[rows(z * 32, 32), :].astype(F32)
        for k in range(1, NZ):
            total += oazr[k - 1].astype(F32)
        go_ref[:, 128:] = total

    arrived(grads_in[0])
    spread(0)
    back_head(0)
    b = b_y(b_g)
    a = a_x(a_g)
    w0 = weight_start(0)
    back_head(1)
    w0 = weight_y(0, w0)
    w1 = weight_start(1)
    arrived(grads_in[1])
    spread(1)
    back_head(2)
    w1 = weight_y(1, w1)
    w2 = weight_start(2)
    arrived(row_z)
    sent(row_z)
    moved(z_to_y(), lambda c: mzr[:, :, c].reshape(256, 256), ms)
    row_y = send_y(ms, myr)
    w0 = weight_z(0, w0)
    b = b_x(b)
    back_head(3)
    w2 = weight_y(2, w2)
    w3 = weight_start(3)
    w1 = weight_z(1, w1)
    w3 = weight_y(3, w3)
    b = b_z(b)
    a = a_y(a)
    w2 = weight_z(2, w2)
    arrived(row_y)
    sent(row_y)
    moved(y_to_g(), lambda c: myr[:, :, c].reshape(256, 256), ms)
    row_g = send_g(ms, mgr)
    weight_end(0, w0)
    w3 = weight_z(3, w3)
    a = a_z(a)
    weight_end(1, w1)
    b_end(b)
    arrived(row_g)
    moved(returning[...], lambda c: mgr[:, :, c].reshape(256, 256), image_ref)
    weight_end(2, w2)
    weight_end(3, w3)
    a_end(a)
    for c in copies.values():
        c.wait_send()
    assert used[0] == n_sems


def shards(
    ny, nt, patches_in, gain_attn, gain_merge, qkv_weight, out_weight, cotangent, patch_counts, block_target
):
    row_count, width = patches_in.shape
    images = patch_counts.shape[0]
    hcols = out_weight.shape[0]
    heads = hcols // HEAD_V
    cols = 3 * HEAD_V
    half, yrows = width // 2, width // 2 // ny
    wide = hcols - 128
    to_all = NZ - 1 + ny - 1 + 1
    n_sems = (
        to_all
        + 2 * (nt - 1)
        + images * (nt - 1)
        + 2 * to_all
        + 2 * (nt - 1)
        + to_all + nt - 1
        + to_all + 2 * nt - 2
        + heads * to_all
    )
    v = pltpu.VMEM
    scratch = [
        v((row_count, width), BF16),
        v((3 * hcols, width), BF16),
        v((256, width), BF16),
        v((256, width), BF16),
        v((width, row_count), BF16),
        v((3 * hcols, row_count), BF16),
        v((images * heads, 256, 256), BF16),
        v((hcols, 256), BF16),
        v((images, 256, hcols), BF16),
        v((nt, 256, hcols), BF16),
        v((nt, hcols, width), BF16),
        v((256, width), F32),
        v((8, 128), I32),
        v((ny, 8, 128), I32),
        v((NZ, ny, 8, 128), I32),
        v((2, NZ, ny, 8, 128), I32),
        v((2, 256, 256), BF16),
        v((256, 256), BF16),
        v((256, width), BF16),
        v((ny, 64, width), BF16),
        v((NZ, 32, width), BF16),
        v((2, 128, width), BF16),
        v((256, width), BF16),
        v((ny, 64, width), BF16),
        v((NZ, 32, width), BF16),
        v((2, 128, width), BF16),
        v((256, width), BF16),
        v((256, width), BF16),
        v((256, width), BF16),
        v((width, 256), BF16),
        v((nt, wide, 256), BF16),
        v((nt, hcols, 256), BF16),
        v((nt, hcols, 256), BF16),
        v((hcols, row_count), BF16),
        v((2, nt, wide, half), BF16),
        v((nt, wide, half), BF16),
        v((nt - 1, wide, half), BF16),
        v((half, wide), BF16),
        v((ny - 1, yrows, wide), BF16),
        v((NZ * 32, wide), BF16),
        v((NZ - 1, 32, wide), BF16),
        v((2, half, nt * 128), BF16),
        v((half, nt * 128), BF16),
        v((ny - 1, yrows, nt * 128), BF16),
        v((nt, yrows, 128), BF16),
        v((nt - 1, yrows, 128), BF16),
        v((NZ * 32, 128), BF16),
        v((NZ - 1, 32, 128), BF16),
        v((heads, width, cols), BF16),
        v((heads, half, cols), BF16),
        v((heads, ny - 1, yrows, cols), BF16),
        v((heads, NZ * 32, cols), BF16),
        v((heads, NZ - 1, 32, cols), BF16),
        pltpu.SemaphoreType.DMA((images + 3,)),
        pltpu.SemaphoreType.DMA((n_sems,)),
        pltpu.SemaphoreType.DMA((n_sems,)),
    ]
    in_vmem = pl.BlockSpec(memory_space=pltpu.VMEM)
    in_hbm = pl.BlockSpec(memory_space=pl.ANY)
    image_rows, gq, go = pl.pallas_call(
        functools.partial(kernel, ny, nt, n_sems),
        out_shape=(
            jax.ShapeDtypeStruct((256, width), BF16),
            jax.ShapeDtypeStruct((heads, 32, cols), F32),
            jax.ShapeDtypeStruct((32, hcols), F32),
        ),
        in_specs=[pl.BlockSpec(memory_space=pltpu.SMEM)] + [in_vmem] * 3 + [in_hbm] * 4,
        out_specs=(in_vmem,) * 3,
        scratch_shapes=scratch,
        compiler_params=pltpu.CompilerParams(
            collective_id=0, has_side_effects=True, vmem_limit_bytes=62 << 20
        ),
        name="block",
    )(
        patch_counts,
        gain_attn,
        gain_merge,
        block_target.reshape(1, -1),
        patches_in,
        qkv_weight.T,
        out_weight,
        cotangent,
    )
    zrows = yrows // NZ
    grad_qkv = jnp.moveaxis(gq[:, :zrows], 0, 1).reshape(zrows, heads * cols)
    grad_out = go[:zrows].T
    return image_rows, grad_qkv, grad_out


def solution(mesh):
    ny, nt = mesh.shape["seq"] // NZ, mesh.shape["tp"]
    return jax.shard_map(
        functools.partial(shards, ny, nt),
        mesh=mesh,
        in_specs=(
            P(("grp", "seq"), None),
            P(),
            P(),
            P(None, "tp"),
            P("tp", None),
            P(("grp", "seq"), "tp"),
            P(("grp", "seq")),
            P(("grp", "seq")),
        ),
        out_specs=(P(("grp", "seq"), "tp"), P(("grp", "seq"), "tp"), P("tp", ("grp", "seq"))),
        check_vma=False,
    )
```

```python
import functools

import jax
import jax.numpy as jnp
from jax import lax
from jax.experimental import pallas as pl
from jax.experimental.pallas import tpu as pltpu
from jax.sharding import PartitionSpec as P

HEAD_V = 80
NZ = 8
F32 = jnp.float32
BF16 = jnp.bfloat16
I32 = jnp.int32
MESH = pl.DeviceIdType.MESH


def mm(a, b):
    return lax.dot_general(a, b, (((1,), (0,)), ((), ())), preferred_element_type=F32)


def mm_t(a, b):
    return lax.dot_general(a, b, (((1,), (1,)), ((), ())), preferred_element_type=F32)


def iota(shape, dim):
    return lax.broadcasted_iota(I32, shape, dim)


def ones_where(cond):
    return jnp.where(cond, 1.0, 0.0)


def norm_parts(values):
    center = values - jnp.mean(values, axis=-1, keepdims=True)
    spread = jnp.mean(center * center, axis=-1, keepdims=True)
    return center, lax.rsqrt(spread + 1e-06)


def kernel(
    ny,
    nt,
    n_sems,
    counts,
    ga_ref,
    gm_ref,
    bt_ref,
    x_hbm,
    wt_hbm,
    ow_hbm,
    cot_hbm,
    image_hbm,
    gq_ref,
    go_ref,
    x_ref,
    wt,
    cot_ref,
    nrm,
    nrmt,
    qkvt,
    probs,
    ot,
    hs,
    hm,
    wf,
    res,
    bts,
    bty,
    btz,
    btg,
    placing,
    returning,
    cs,
    cyr,
    czr,
    cgr,
    ms,
    myr,
    mzr,
    mgr,
    inc,
    image,
    merged,
    gown,
    gownt,
    hmt,
    ghs,
    ghr,
    ght,
    oa,
    oag,
    oax,
    oay,
    oayr,
    oaz,
    oazr,
    ob,
    obg,
    obyr,
    obx,
    obxr,
    obz,
    obzr,
    dws,
    dgr,
    dyr,
    dz,
    dzr,
    lsem,
    ssem,
    rsem,
):
    g = lax.axis_index("grp")
    s = lax.axis_index("seq")
    t = lax.axis_index("tp")
    y = lax.div(s, NZ)
    z = lax.rem(s, NZ)
    images = x_ref.shape[0] // 256
    width = x_ref.shape[1]
    hcols = wt.shape[0] // 3
    heads = hcols // HEAD_V
    half = width // 2
    yrows = half // ny
    zrows = yrows // NZ

    def at_z(k):
        return lax.rem(z + k, NZ)

    def at_y(k):
        return lax.rem(y + k, ny)

    def at_t(k):
        return lax.rem(t + k, nt)

    def dev_z(k):
        return {"seq": y * NZ + at_z(k)}

    def dev_y(k):
        return {"seq": at_y(k) * NZ + z}

    def dev_t(k):
        return {"tp": at_t(k)}

    dev_g = {"grp": 1 - g}
    to_t = (1, 3, 2)

    used = [0]
    open_sends = {}

    class Group:
        def __init__(self, whole):
            self.k = used[0]
            used[0] += 1
            self.whole = self.copy(whole, whole, dev_g)
            open_sends[self.k] = self

        def copy(self, src, dst, device):
            return pltpu.make_async_remote_copy(
                src_ref=src,
                dst_ref=dst,
                send_sem=ssem.at[self.k],
                recv_sem=rsem.at[self.k],
                device_id=device,
                device_id_type=MESH,
            )

        def push(self, src, dst, device):
            self.copy(src, dst, device).start()
            return self

        def arrived(self):
            self.whole.wait_recv()

        def sent(self):
            self.whole.wait_send()
            del open_sends[self.k]

    def push_all(whole, pieces):
        group = Group(whole)
        for piece in pieces:
            group.push(*piece)
        return group

    def rows(start, size):
        return pl.ds(pl.multiple_of(start, size if size & (size - 1) == 0 else 16), size)

    barrier = pltpu.get_barrier_semaphore()
    partners = (
        [dev_z(k) for k in range(1, NZ)]
        + [dev_y(k) for k in range(1, ny)]
        + [dev_t(k) for k in range(1, nt)]
        + [dev_g]
    )
    for device in partners:
        pl.semaphore_signal(barrier, inc=1, device_id=device, device_id_type=MESH)

    def image_rows_of(i):
        at = pl.ds(i * 256, 256)
        return pltpu.make_async_copy(x_hbm.at[at, :], x_ref.at[at, :], lsem.at[i])

    loads_x = [image_rows_of(i) for i in range(images)]
    load_w = pltpu.make_async_copy(wt_hbm, wt, lsem.at[images])
    load_c = pltpu.make_async_copy(cot_hbm, cot_ref, lsem.at[images + 1])
    load_o = pltpu.make_async_copy(ow_hbm, wf.at[t], lsem.at[images + 2])
    loads_x[0].start()
    load_w.start()
    load_c.start()

    for load in loads_x[1:]:
        load.start()
    load_o.start()
    hrows = hcols // 2
    own_half = pl.ds(pl.multiple_of(g * hrows, 16), hrows)
    eye = ones_where(iota((256, 256), 0) == iota((256, 256), 1)).astype(BF16)
    bt_row = bt_ref[...]
    bts[...] = jnp.broadcast_to(bt_row, bts.shape)
    gain_a = ga_ref[...].reshape(1, width)
    gain_m = gm_ref[...].reshape(1, width)

    def forward_norm(i):
        base = i * 256
        loads_x[i].wait()

        def norm_rows(c, _):
            at = pl.ds(pl.multiple_of(c * 32, 32), 32)
            values = x_ref[pl.ds(pl.multiple_of(base + c * 32, 32), 32), :].astype(F32)
            center, scale = norm_parts(values)
            nrm[at, :] = (center * scale * gain_a).astype(BF16)
            return 0

        lax.fori_loop(0, 8, norm_rows, 0)
        own = ones_where(iota((64, 256), 1) == 4 * iota((64, 256), 0) + t).astype(BF16)
        res[base // 4 : base // 4 + 64, :] = mm(own, x_ref[base : base + 256, :])
        for f in range(width // 256):
            nrmt[f * 256 : (f + 1) * 256, base : base + 256] = mm_t(
                eye, nrm[:, f * 256 : (f + 1) * 256]
            ).astype(BF16)

    def forward_qkv(i):
        base = i * 256
        if i == 0:
            load_w.wait()

        def project(c, _):
            at = pl.ds(pl.multiple_of(c * 240, 16), 240)
            qkvt[at, base : base + 256] = mm_t(wt[at, :], nrm[...]).astype(BF16)
            return 0

        lax.fori_loop(0, 3 * hcols // 240, project, 0)

    def forward_attend(i):
        base = i * 256
        live = iota((256, 128), 0) < counts[i]
        cols = pl.ds(base, 256)
        for h in range(heads):
            row = h * 3 * HEAD_V
            k = mm_t(eye, qkvt[row + HEAD_V : row + 2 * HEAD_V, cols]).astype(BF16)
            v_t = qkvt[row + 2 * HEAD_V : row + 3 * HEAD_V, cols]
            for c in range(2):
                lanes = slice(c * 128, (c + 1) * 128)
                q_t = qkvt[row : row + HEAD_V, pl.ds(base + c * 128, 128)]
                scores = mm(k, q_t) * HEAD_V**-0.5
                scores = jnp.where(live, scores, -1e30)
                weights = jnp.exp(scores - jnp.max(scores, axis=0, keepdims=True))
                weights = weights * (1.0 / jnp.sum(weights, axis=0, keepdims=True))
                weights = weights.astype(BF16)
                probs[i * heads + h, :, lanes] = weights
                ot[h * HEAD_V : (h + 1) * HEAD_V, lanes] = mm(v_t, weights).astype(BF16)
        by_patch = ones_where(
            iota((256, 256), 1) == 4 * (iota((256, 256), 0) & 63) + (iota((256, 256), 0) >> 6)
        ).astype(BF16)
        hs[i] = mm_t(by_patch, ot[...]).astype(BF16)

    def send_heads(i):
        out = pl.ds(i * 64, 64)
        for k in to_t:
            heads_in.push(hs.at[i, rows(at_t(k) * 64, 64), :], hm.at[t, out, :], dev_t(k))
        hm[pl.ds(t, 1), out, :] = hs[i, rows(t * 64, 64), :][None]

    row_i, lane_i = iota((256, 256), 0), iota((256, 256), 1)

    def z_to_y():
        return ones_where(
            lane_i == ((row_i >> 3) & (NZ - 1)) * 32 + (row_i >> 6) * 8 + (row_i & 7)
        ).astype(BF16)

    def y_to_g():
        return ones_where(
            lane_i
            == ((row_i >> 5) & (ny - 1)) * 64
            + ((row_i >> 2) & (NZ - 1)) * 8
            + (row_i >> 7) * 4
            + (row_i & 3)
        ).astype(BF16)

    def g_to_z():
        return ones_where(
            lane_i
            == ((row_i >> 2) & 1) * 128
            + ((row_i >> 3) & (ny - 1)) * 32
            + (row_i >> 5) * 4
            + (row_i & 3)
        ).astype(BF16)

    def y_to_z():
        return ones_where(
            lane_i == ((row_i >> 3) & (ny - 1)) * 64 + (row_i >> 5) * 8 + (row_i & 7)
        ).astype(BF16)

    def z_to_g():
        return ones_where(
            lane_i
            == ((row_i >> 2) & (NZ - 1)) * 32
            + ((row_i >> 5) & (ny - 1)) * 8
            + (row_i >> 7) * 4
            + (row_i & 3)
        ).astype(BF16)

    hw = width // 2

    def send_y(buf, dst):
        group = push_all(
            dst.at[pl.ds(0, ny - 1)],
            [(buf.at[rows(at_y(k) * 64, 64), :], dst.at[y], dev_y(k)) for k in (1, 3, 2)],
        )
        dst[pl.ds(y, 1)] = buf[rows(y * 64, 64), :][None]
        return group

    def send_z(buf, dst):
        group = push_all(
            dst.at[pl.ds(0, NZ - 1)],
            [
                (buf.at[rows(at_z(k) * 32, 32), :], dst.at[z], dev_z(k))
                for k in (4, 3, 5, 2, 6, 1, 7)
            ],
        )
        dst[pl.ds(z, 1)] = buf[rows(z * 32, 32), :][None]
        return group

    def send_g(buf, dst):
        group = push_all(
            dst.at[0], [(buf.at[rows((1 - g) * 128, 128), :], dst.at[g], dev_g)]
        )
        dst[pl.ds(g, 1)] = buf[rows(g * 128, 128), :][None]
        return group

    class Exchange:
        def __init__(self, buf, from_y, from_z, from_g):
            self.buf, self.from_y, self.from_z, self.from_g = buf, from_y, from_z, from_g
            self.group = [None, None]

        def begin(self, order, src):
            for j in range(2):
                if j:
                    order = mm(z_to_y(), order).astype(BF16)
                self.buf[j] = mm(order, src[:, j * hw : (j + 1) * hw]).astype(BF16)
                send, to = ((send_z, self.from_z), (send_y, self.from_y))[j]
                self.group[j] = send(self.buf.at[j], to.at[j])

        def next(self, j, came, order, send, to):
            self.group[j].arrived()
            self.group[j].sent()
            self.buf[j] = mm(order(), came[j].reshape(256, hw)).astype(BF16)
            self.group[j] = send(self.buf.at[j], to.at[j])

        def second(self, j):
            if j == 0:
                self.next(0, self.from_z, z_to_y, send_y, self.from_y)
            else:
                self.next(1, self.from_y, y_to_z, send_z, self.from_z)

        def third(self, j):
            if j == 0:
                self.next(0, self.from_y, y_to_g, send_g, self.from_g)
            else:
                self.next(1, self.from_z, z_to_g, send_g, self.from_g)

        def end(self, order, dst):
            for j in range(2):
                self.group[j].arrived()
                dst[:, j * hw : (j + 1) * hw] = mm(
                    order, self.from_g[j].reshape(256, hw)
                ).astype(BF16)

    forward_norm(0)
    forward_qkv(0)
    forward_attend(0)

    pair = iota((256, 128), 0)
    block_lane = iota((256, 128), 1)
    target = jnp.broadcast_to(bt_row, (256, 128)).astype(F32)
    target_of = jnp.sum(jnp.where(block_lane == (pair >> 1), target, 0.0), axis=1, keepdims=True)
    target_of = target_of.astype(I32)
    shard_of = target_of >> 7
    earlier = ((jnp.broadcast_to(bt_row, (256, 128)) >> 7) == shard_of) & (block_lane < (pair >> 1))
    rank_of = jnp.sum(ones_where(earlier), axis=1, keepdims=True).astype(I32)
    row_of = rank_of * 2 + (iota((256, 1), 0) & 1)
    s_g, s_y, s_z = shard_of >> 5, (shard_of >> 3) & (ny - 1), shard_of & (NZ - 1)
    placing[0] = ones_where(lane_i == shard_of * 4 + row_of).astype(BF16)
    to_at = (s_z * 32 + s_y * 8 + s_g * 4 + row_of).astype(F32)
    to_row = jnp.sum(jnp.where(row_i == lane_i, to_at, 0.0), axis=0, keepdims=True).astype(I32)
    placing[1] = ones_where(row_i == to_row).astype(BF16)

    pl.semaphore_wait(barrier, len(partners))

    slots_y = push_all(
        bty.at[pl.ds(0, ny - 1)], [(bts, bty.at[y], dev_y(k)) for k in range(1, ny)]
    )
    weight_part = wf.at[pl.ds(0, nt - 1), pl.ds(0, hrows), :]
    weight_t = push_all(
        weight_part,
        [(ow_hbm.at[own_half, :], wf.at[t, own_half, :], dev_t(k)) for k in to_t],
    )
    heads_in = Group(hm.at[pl.ds(0, nt - 1)])
    send_heads(0)
    bty[pl.ds(y, 1)] = bts[...][None]

    forward_norm(1)
    slots_y.arrived()
    slots_z = push_all(
        btz.at[pl.ds(0, NZ - 1)], [(bty, btz.at[z], dev_z(k)) for k in range(1, NZ)]
    )
    btz[pl.ds(z, 1)] = bty[...][None]
    forward_qkv(1)
    slots_z.arrived()
    slots_g = push_all(btg.at[0], [(btz, btg.at[g], dev_g)])
    btg[pl.ds(g, 1)] = btz[...][None]
    load_c.wait()
    slots_g.arrived()
    lanes3 = (ny * NZ, 8, 128)
    sub3 = iota(lanes3, 1)
    both = jnp.where(sub3 < 4, btg[0].reshape(lanes3), btg[1].reshape(lanes3))
    hit = (both >> 7) == (g * ny * NZ + s)
    slot = (both & 127).astype(F32)
    lane3 = iota(lanes3, 2).astype(F32)
    first_lane = jnp.min(jnp.where(hit, lane3, 999.0), axis=2, keepdims=True)
    slot_0 = jnp.sum(jnp.where(hit & (lane3 == first_lane), slot, 0.0), axis=2, keepdims=True)
    slot_1 = jnp.sum(jnp.where(hit & (lane3 != first_lane), slot, 0.0), axis=2, keepdims=True)
    sub1 = iota((ny * NZ, 8, 1), 1)
    slot_row = jnp.where((sub1 & 2) == 2, slot_1, slot_0) * 2.0 + (sub1 & 1).astype(F32)
    slot_row = slot_row.reshape(256, 1)
    cot = Exchange(cs, cyr, czr, cgr)
    cot.begin(ones_where(lane_i.astype(F32) == slot_row).astype(BF16), cot_ref)
    slot_lane = jnp.sum(jnp.where(row_i == lane_i, slot_row, 0.0), axis=0, keepdims=True)
    back_at = ones_where(row_i.astype(F32) == slot_lane).astype(BF16)
    returning[...] = mm(back_at, g_to_z()).astype(BF16)

    forward_attend(1)
    send_heads(1)
    forward_norm(2)
    forward_qkv(2)
    cot.second(1)
    forward_attend(2)
    send_heads(2)
    forward_norm(3)
    forward_qkv(3)
    cot.second(0)
    forward_attend(3)
    send_heads(3)
    weight_t.arrived()
    weight_g = push_all(
        weight_part,
        [
            (wf.at[at_t(nt - k), own_half, :], wf.at[at_t(nt - k), own_half, :], dev_g)
            for k in to_t
        ],
    )
    load_o.wait()
    cot.third(0)
    heads_in.arrived()
    wide = hcols - 128
    for q in range(nt):
        hmt[q] = mm_t(eye[:wide, :wide], hm[q, :, 128:]).astype(BF16)
    cot.third(1)
    weight_g.arrived()

    def project_out(c, _):
        cols = pl.ds(pl.multiple_of(c * 256, 256), 256)
        total = res[:, cols]
        for q in range(nt):
            total += mm(hm[q], wf[q, :, cols])
        res[:, cols] = total
        return 0

    lax.fori_loop(0, width // 256, project_out, 0)
    cot.end(placing[0], inc)

    def merge_rows(c, _):
        at = pl.ds(pl.multiple_of(c * 32, 32), 32)
        center, scale = norm_parts(res[at, :])
        hat = center * scale
        alive = ones_where(4 * ((iota((32, 1), 0) + c * 32) & 63) < counts[lax.div(c, 2)])
        merged[at, :] = (hat * gain_m * alive).astype(BF16)
        grad = inc[at, :].astype(F32) * alive * gain_m
        mean_grad = jnp.mean(grad, axis=-1, keepdims=True)
        mean_hat = jnp.mean(grad * hat, axis=-1, keepdims=True)
        gown[at, :] = (scale * (grad - mean_grad - hat * mean_hat)).astype(BF16)
        return 0

    lax.fori_loop(0, 8, merge_rows, 0)

    pairs = 2
    prows = hcols // pairs
    for k in to_t + (0,):
        q = at_t(k)
        ghs[pl.ds(q, 1)] = mm_t(wf[pl.ds(q, 1)].reshape(hcols, width), gown[...]).astype(BF16)[None]
    grads_in = [
        push_all(
            ghr.at[pl.ds(0, nt - 1), pl.ds(0, prows), :],
            [
                (
                    ghs.at[at_t(k), pl.ds(j * prows, prows), :],
                    ghr.at[t, pl.ds(j * prows, prows), :],
                    dev_t(k),
                )
                for k in to_t
            ],
        )
        for j in range(pairs)
    ]
    ghr[pl.ds(t, 1)] = ghs[pl.ds(t, 1)]

    row = Exchange(ms, myr, mzr, mgr)
    row.begin(placing[1], merged)

    for f in range(width // 256):
        gownt[f * 256 : (f + 1) * 256, :] = mm_t(eye, gown[:, f * 256 : (f + 1) * 256]).astype(BF16)
    def terms_b(side):
        def one(c, _):
            at = pl.ds(pl.multiple_of(side * half + c * (half // 2), 64), half // 2)
            to = pl.ds(pl.multiple_of(c * (half // 2), 64), half // 2)
            for q in range(nt):
                ob[pl.ds(side, 1), to, q * 128 : (q + 1) * 128] = mm(
                    gownt[at, :], hm[q, :, :128]
                ).astype(BF16)[None]
            return 0

        lax.fori_loop(0, 2, one, 0)

    def terms_a(side, k):
        cols = pl.ds(pl.multiple_of(side * half, 128), half)
        q = at_t(k)
        value = mm(hmt[pl.ds(q, 1)].reshape(wide, 256), gown[:, cols])
        oa[pl.ds(side, 1), pl.ds(q, 1)] = value.astype(BF16)[None, None]

    terms_b(1 - g)
    b = push_all(obg, [(ob.at[1 - g], obg, dev_g)])
    a = []
    for k in to_t + (0,):
        terms_a(1 - g, k)
        a.append(push_all(oag.at[0], [(oa.at[1 - g, at_t(k)], oag.at[at_t(k)], dev_g)]))
    terms_b(g)

    def spread(j):
        def one(i, _):
            cols = pl.ds(pl.multiple_of(i * 256, 256), 256)
            total = jnp.zeros((prows, 256), F32)
            for p in range(nt):
                order = ones_where(lane_i == 4 * (row_i - 64 * i) + p).astype(BF16)
                total += mm(ghr[p, j * prows : (j + 1) * prows, :], order)
            ght[j * prows : (j + 1) * prows, cols] = total.astype(BF16)
            return 0

        lax.fori_loop(0, images, one, 0)

    def back_head(h):
        row = h * 3 * HEAD_V

        def back_image(i, _):
            cols = pl.ds(pl.multiple_of(i * 256, 256), 256)
            at_q, at_k, at_v = row, row + HEAD_V, row + 2 * HEAD_V
            q_t = qkvt[at_q : at_q + HEAD_V, cols]
            k_t = qkvt[at_k : at_k + HEAD_V, cols]
            v_t = qkvt[at_v : at_v + HEAD_V, cols]
            d_t = ght[h * HEAD_V : (h + 1) * HEAD_V, cols]
            v = mm_t(eye, v_t).astype(BF16)
            weights = probs[i * heads + h]
            grad_v = mm_t(d_t, weights).astype(BF16)
            parts = []
            for c in range(2):
                lanes = slice(c * 128, (c + 1) * 128)
                w = weights[:, lanes].astype(F32)
                grad_w = mm(v, d_t[:, lanes]).astype(BF16).astype(F32)
                inner = jnp.sum(w * grad_w, axis=0, keepdims=True)
                parts.append((w * (grad_w - inner) * HEAD_V**-0.5).astype(BF16))
            grad_s = jnp.concatenate(parts, axis=1)
            grad_q = mm(k_t, grad_s).astype(BF16)
            grad_k = mm_t(q_t, grad_s).astype(BF16)
            qkvt[at_q : at_q + HEAD_V, cols] = grad_q
            qkvt[at_k : at_k + HEAD_V, cols] = grad_k
            qkvt[at_v : at_v + HEAD_V, cols] = grad_v
            return 0

        lax.fori_loop(0, images, back_image, 0)

    def weight_terms(h, side):
        def one(c, _):
            at = pl.ds(pl.multiple_of(side * half + c * (half // 2), 64), half // 2)
            dws[h, at, :] = mm_t(
                nrmt[at, :], qkvt[h * 3 * HEAD_V : (h + 1) * 3 * HEAD_V, :]
            ).astype(BF16)
            return 0

        lax.fori_loop(0, 2, one, 0)

    def to_shards():
        r, c = iota((NZ * 32, yrows), 0), iota((NZ * 32, yrows), 1)
        return ones_where((c == (r >> 5) * zrows + (r & 31)) & ((r & 31) < zrows)).astype(BF16)

    def add(a, b):
        return a.astype(F32) + b.astype(F32)

    their_rows = pl.ds(pl.multiple_of((1 - g) * half, 128), half)
    own_rows = pl.ds(pl.multiple_of(g * half, 128), half)
    order_y = [(k, k - 1) for k in (1, 3, 2)]
    order_z = [(k, k - 1) for k in (4, 3, 5, 2, 6, 1, 7)]

    def rows_y(k):
        return pl.ds(pl.multiple_of(at_y(k) * yrows, 16), yrows)

    def weight_start(h):
        weight_terms(h, 1 - g)
        group = push_all(dgr.at[h], [(dws.at[h, their_rows, :], dgr.at[h], dev_g)])
        weight_terms(h, g)
        return group

    def weight_y(h, group):
        group.arrived()
        dgr[h] = add(dws[h, own_rows, :], dgr[h]).astype(BF16)
        return push_all(
            dyr.at[h], [(dgr.at[h, rows_y(k), :], dyr.at[h, j], dev_y(k)) for k, j in order_y]
        )

    def weight_z(h, group):
        group.arrived()
        total = dgr[h, rows_y(0), :].astype(F32)
        for k in range(1, ny):
            total += dyr[h, k - 1].astype(F32)
        dz[h] = mm(to_shards(), total.astype(BF16)).astype(BF16)
        return push_all(
            dzr.at[h],
            [(dz.at[h, rows(at_z(k) * 32, 32), :], dzr.at[h, j], dev_z(k)) for k, j in order_z],
        )

    def weight_end(h, group):
        group.arrived()
        total = dz[h, rows(z * 32, 32), :].astype(F32)
        for k in range(1, NZ):
            total += dzr[h, k - 1].astype(F32)
        gq_ref[:, h * 3 * HEAD_V : (h + 1) * 3 * HEAD_V] = total[:zrows]

    def b_y(group):
        group.arrived()
        obg[...] = add(ob[pl.ds(g, 1)].reshape(half, nt * 128), obg[...]).astype(BF16)
        return push_all(obyr, [(obg.at[rows_y(k), :], obyr.at[j], dev_y(k)) for k, j in order_y])

    def b_x(group):
        group.arrived()
        total = obg[rows_y(0), :].astype(F32)
        for k in range(1, ny):
            total += obyr[k - 1].astype(F32)
        for q in range(nt):
            obx[q] = total[:, q * 128 : (q + 1) * 128].astype(BF16)
        return push_all(obxr, [(obx.at[at_t(k)], obxr.at[k - 1], dev_t(k)) for k in to_t])

    def b_z(group):
        group.arrived()
        total = obx[pl.ds(t, 1)].reshape(yrows, 128).astype(F32)
        for k in range(1, nt):
            total += obxr[k - 1].astype(F32)
        obz[...] = mm(to_shards(), total.astype(BF16)).astype(BF16)
        return push_all(
            obzr, [(obz.at[rows(at_z(k) * 32, 32), :], obzr.at[j], dev_z(k)) for k, j in order_z]
        )

    def b_end(group):
        group.arrived()
        total = obz[rows(z * 32, 32), :].astype(F32)
        for k in range(1, NZ):
            total += obzr[k - 1].astype(F32)
        go_ref[:, :128] = total[:zrows]

    def a_x(groups):
        out = Group(oax)
        for k, group in zip(to_t + (0,), groups):
            group.arrived()
            q = at_t(k)
            mine = oa[pl.ds(g, 1), pl.ds(q, 1)].reshape(wide, half)
            oag[pl.ds(q, 1)] = add(mine, oag[pl.ds(q, 1)].reshape(wide, half)).astype(BF16)[None]
            if k:
                out.push(oag.at[q], oax.at[k - 1], dev_t(k))
        return out

    def a_y(group):
        group.arrived()
        for f in range(half // 128):
            cols = slice(f * 128, (f + 1) * 128)
            total = oag[pl.ds(t, 1), :, cols].reshape(wide, 128).astype(F32)
            for k in range(1, nt):
                total += oax[k - 1, :, cols].astype(F32)
            oay[cols, :] = mm_t(eye[:128, :128], total.astype(BF16)).astype(BF16)
        return push_all(oayr, [(oay.at[rows_y(k), :], oayr.at[j], dev_y(k)) for k, j in order_y])

    def a_z(group):
        group.arrived()
        total = oay[rows_y(0), :].astype(F32)
        for k in range(1, ny):
            total += oayr[k - 1].astype(F32)
        oaz[...] = mm(to_shards(), total.astype(BF16)).astype(BF16)
        return push_all(
            oazr, [(oaz.at[rows(at_z(k) * 32, 32), :], oazr.at[j], dev_z(k)) for k, j in order_z]
        )

    def a_end(group):
        group.arrived()
        total = oaz[rows(z * 32, 32), :].astype(F32)
        for k in range(1, NZ):
            total += oazr[k - 1].astype(F32)
        go_ref[:, 128:] = total[:zrows]

    b = b_y(b)
    for k in to_t + (0,):
        terms_a(g, k)
    grads_in[0].arrived()
    spread(0)
    back_head(0)
    a = a_x(a)
    w0 = weight_start(0)
    row.second(1)
    back_head(1)
    w0 = weight_y(0, w0)
    row.second(0)
    w1 = weight_start(1)
    grads_in[1].arrived()
    spread(1)
    b = b_x(b)
    back_head(2)
    w1 = weight_y(1, w1)
    w2 = weight_start(2)
    w0 = weight_z(0, w0)
    b = b_z(b)
    back_head(3)
    w2 = weight_y(2, w2)
    w3 = weight_start(3)
    w1 = weight_z(1, w1)
    row.third(0)
    w3 = weight_y(3, w3)
    a = a_y(a)
    row.third(1)
    w2 = weight_z(2, w2)
    weight_end(0, w0)
    b_end(b)
    w3 = weight_z(3, w3)
    row.end(returning[...], image)
    store_i = pltpu.make_async_copy(image, image_hbm, lsem.at[images + 3])
    store_i.start()
    a = a_z(a)
    weight_end(1, w1)
    weight_end(2, w2)
    weight_end(3, w3)
    a_end(a)
    store_i.wait()
    for group in list(open_sends.values()):
        group.sent()
    assert used[0] == n_sems


def hand_over(a, b, c, a_out, b_out, c_out):
    a_out[...] = a[...]
    b_out[...] = b[...]
    c_out[...] = c[...]


def shards(
    ny, nt, patches_in, gain_attn, gain_merge, qkv_weight, out_weight, cotangent, patch_counts, block_target
):
    row_count, width = patches_in.shape
    images = patch_counts.shape[0]
    hcols = out_weight.shape[0]
    heads = hcols // HEAD_V
    cols = 3 * HEAD_V
    half, yrows = width // 2, width // 2 // ny
    wide = hcols - 128
    zrows = yrows // NZ
    n_sems = 3 + 2 + 1 + 6 + 6 + 2 + 4 + (nt + 3) + 3 * heads
    v = pltpu.VMEM
    scratch = [
        v((row_count, width), BF16),
        v((3 * hcols, width), BF16),
        v((256, width), BF16),
        v((256, width), BF16),
        v((width, row_count), BF16),
        v((3 * hcols, row_count), BF16),
        v((images * heads, 256, 256), BF16),
        v((hcols, 256), BF16),
        v((images, 256, hcols), BF16),
        v((nt, 256, hcols), BF16),
        v((nt, hcols, width), BF16),
        v((256, width), F32),
        v((8, 128), I32),
        v((ny, 8, 128), I32),
        v((NZ, ny, 8, 128), I32),
        v((2, NZ, ny, 8, 128), I32),
        v((2, 256, 256), BF16),
        v((256, 256), BF16),
        v((2, 256, half), BF16),
        v((2, ny, 64, half), BF16),
        v((2, NZ, 32, half), BF16),
        v((2, 2, 128, half), BF16),
        v((2, 256, half), BF16),
        v((2, ny, 64, half), BF16),
        v((2, NZ, 32, half), BF16),
        v((2, 2, 128, half), BF16),
        v((256, width), BF16),
        v((256, width), BF16),
        v((256, width), BF16),
        v((256, width), BF16),
        v((width, 256), BF16),
        v((nt, wide, 256), BF16),
        v((nt, hcols, 256), BF16),
        v((nt, hcols, 256), BF16),
        v((hcols, row_count), BF16),
        v((2, nt, wide, half), BF16),
        v((nt, wide, half), BF16),
        v((nt - 1, wide, half), BF16),
        v((half, wide), BF16),
        v((ny - 1, yrows, wide), BF16),
        v((NZ * 32, wide), BF16),
        v((NZ - 1, 32, wide), BF16),
        v((2, half, nt * 128), BF16),
        v((half, nt * 128), BF16),
        v((ny - 1, yrows, nt * 128), BF16),
        v((nt, yrows, 128), BF16),
        v((nt - 1, yrows, 128), BF16),
        v((NZ * 32, 128), BF16),
        v((NZ - 1, 32, 128), BF16),
        v((heads, width, cols), BF16),
        v((heads, half, cols), BF16),
        v((heads, ny - 1, yrows, cols), BF16),
        v((heads, NZ * 32, cols), BF16),
        v((heads, NZ - 1, 32, cols), BF16),
        pltpu.SemaphoreType.DMA((images + 4,)),
        pltpu.SemaphoreType.DMA((n_sems,)),
        pltpu.SemaphoreType.DMA((n_sems,)),
    ]
    in_vmem = pl.BlockSpec(memory_space=pltpu.VMEM)
    in_hbm = pl.BlockSpec(memory_space=pl.ANY)
    image_rows, gq, go = pl.pallas_call(
        functools.partial(kernel, ny, nt, n_sems),
        out_shape=(
            jax.ShapeDtypeStruct((256, width), BF16),
            jax.ShapeDtypeStruct((zrows, heads * cols), F32),
            jax.ShapeDtypeStruct((zrows, hcols), F32),
        ),
        in_specs=[pl.BlockSpec(memory_space=pltpu.SMEM)] + [in_vmem] * 3 + [in_hbm] * 4,
        out_specs=(in_hbm, in_vmem, in_vmem),
        scratch_shapes=scratch,
        compiler_params=pltpu.CompilerParams(
            collective_id=0, has_side_effects=True, vmem_limit_bytes=62 << 20
        ),
        name="block",
    )(
        patch_counts,
        gain_attn,
        gain_merge,
        block_target.reshape(1, -1),
        patches_in,
        qkv_weight.T,
        out_weight,
        cotangent,
    )
    image_rows, grad_qkv, grad_out = pl.pallas_call(
        hand_over,
        out_shape=tuple(jax.ShapeDtypeStruct(a.shape, a.dtype) for a in (image_rows, gq, go)),
        in_specs=[in_vmem] * 3,
        out_specs=(in_vmem,) * 3,
        name="hand_over",
    )(image_rows, gq, go)
    return image_rows, grad_qkv, grad_out.T


def solution(mesh):
    ny, nt = mesh.shape["seq"] // NZ, mesh.shape["tp"]
    return jax.shard_map(
        functools.partial(shards, ny, nt),
        mesh=mesh,
        in_specs=(
            P(("grp", "seq"), None),
            P(),
            P(),
            P(None, "tp"),
            P("tp", None),
            P(("grp", "seq"), "tp"),
            P(("grp", "seq")),
            P(("grp", "seq")),
        ),
        out_specs=(P(("grp", "seq"), "tp"), P(("grp", "seq"), "tp"), P("tp", ("grp", "seq"))),
        check_vma=False,
    )
```

```python
import functools

import jax
import jax.numpy as jnp
from jax import lax
from jax.experimental import pallas as pl
from jax.experimental.pallas import tpu as pltpu
from jax.sharding import PartitionSpec as P

HEAD_V = 80
NZ = 8
F32 = jnp.float32
BF16 = jnp.bfloat16
I32 = jnp.int32
MESH = pl.DeviceIdType.MESH


def mm(a, b):
    return lax.dot_general(a, b, (((1,), (0,)), ((), ())), preferred_element_type=F32)


def mm_t(a, b):
    return lax.dot_general(a, b, (((1,), (1,)), ((), ())), preferred_element_type=F32)


def iota(shape, dim):
    return lax.broadcasted_iota(I32, shape, dim)


def ones_where(cond):
    return jnp.where(cond, 1.0, 0.0)


def norm_parts(values):
    center = values - jnp.mean(values, axis=-1, keepdims=True)
    spread = jnp.mean(center * center, axis=-1, keepdims=True)
    return center, lax.rsqrt(spread + 1e-06)


def kernel(
    ny,
    nt,
    n_sems,
    counts,
    ga_ref,
    gm_ref,
    bt_ref,
    x_hbm,
    wt_hbm,
    ow_hbm,
    cot_hbm,
    image_hbm,
    gq_ref,
    go_ref,
    x_ref,
    wt,
    cot_ref,
    nrm,
    nrmt,
    qkvt,
    probs,
    ot,
    hs,
    hm,
    wf,
    res,
    bts,
    bty,
    btz,
    btg,
    placing,
    returning,
    cs,
    cyr,
    czr,
    cgr,
    ms,
    myr,
    mzr,
    mgr,
    inc,
    image,
    merged,
    gown,
    gownt,
    hmt,
    ghs,
    ghr,
    ght,
    oa,
    oag,
    oax,
    oay,
    oayr,
    oaz,
    oazr,
    ob,
    obg,
    obyr,
    obx,
    obxr,
    obz,
    obzr,
    dws,
    dgr,
    dyr,
    dz,
    dzr,
    lsem,
    ssem,
    rsem,
):
    g = lax.axis_index("grp")
    s = lax.axis_index("seq")
    t = lax.axis_index("tp")
    y = lax.div(s, NZ)
    z = lax.rem(s, NZ)
    images = x_ref.shape[0] // 256
    width = x_ref.shape[1]
    hcols = wt.shape[0] // 3
    heads = hcols // HEAD_V
    half = width // 2
    yrows = half // ny
    zrows = yrows // NZ

    def at_z(k):
        return lax.rem(z + k, NZ)

    def at_y(k):
        return lax.rem(y + k, ny)

    def at_t(k):
        return lax.rem(t + k, nt)

    def dev_z(k):
        return {"seq": y * NZ + at_z(k)}

    def dev_y(k):
        return {"seq": at_y(k) * NZ + z}

    def dev_t(k):
        return {"tp": at_t(k)}

    dev_g = {"grp": 1 - g}
    to_t = (1, 3, 2)

    used = [0]
    open_sends = {}

    class Group:
        def __init__(self, whole):
            self.k = used[0]
            used[0] += 1
            self.whole = self.copy(whole, whole, dev_g)
            open_sends[self.k] = self

        def copy(self, src, dst, device):
            return pltpu.make_async_remote_copy(
                src_ref=src,
                dst_ref=dst,
                send_sem=ssem.at[self.k],
                recv_sem=rsem.at[self.k],
                device_id=device,
                device_id_type=MESH,
            )

        def push(self, src, dst, device):
            self.copy(src, dst, device).start()
            return self

        def arrived(self):
            self.whole.wait_recv()

        def sent(self):
            self.whole.wait_send()
            del open_sends[self.k]

    def push_all(whole, pieces):
        group = Group(whole)
        for piece in pieces:
            group.push(*piece)
        return group

    def rows(start, size):
        return pl.ds(pl.multiple_of(start, size if size & (size - 1) == 0 else 16), size)

    barrier = pltpu.get_barrier_semaphore()
    partners = (
        [dev_z(k) for k in range(1, NZ)]
        + [dev_y(k) for k in range(1, ny)]
        + [dev_t(k) for k in range(1, nt)]
        + [dev_g]
    )
    for device in partners:
        pl.semaphore_signal(barrier, inc=1, device_id=device, device_id_type=MESH)

    def image_rows_of(i):
        at = pl.ds(i * 256, 256)
        return pltpu.make_async_copy(x_hbm.at[at, :], x_ref.at[at, :], lsem.at[i])

    loads_x = [image_rows_of(i) for i in range(images)]
    load_w = pltpu.make_async_copy(wt_hbm, wt, lsem.at[images])
    load_c = pltpu.make_async_copy(cot_hbm, cot_ref, lsem.at[images + 1])
    load_o = pltpu.make_async_copy(ow_hbm, wf.at[t], lsem.at[images + 2])
    loads_x[0].start()
    load_w.start()
    load_c.start()

    for load in loads_x[1:]:
        load.start()
    load_o.start()
    hrows = hcols // 2
    own_half = pl.ds(pl.multiple_of(g * hrows, 16), hrows)
    eye = ones_where(iota((256, 256), 0) == iota((256, 256), 1)).astype(BF16)
    bt_row = bt_ref[...]
    bts[...] = jnp.broadcast_to(bt_row, bts.shape)
    gain_a = ga_ref[...].reshape(1, width)
    gain_m = gm_ref[...].reshape(1, width)

    def forward_norm(i):
        base = i * 256
        loads_x[i].wait()

        def norm_rows(c, _):
            at = pl.ds(pl.multiple_of(c * 32, 32), 32)
            values = x_ref[pl.ds(pl.multiple_of(base + c * 32, 32), 32), :].astype(F32)
            center, scale = norm_parts(values)
            nrm[at, :] = (center * scale * gain_a).astype(BF16)
            return 0

        lax.fori_loop(0, 8, norm_rows, 0, unroll=2)
        own = ones_where(iota((64, 256), 1) == 4 * iota((64, 256), 0) + t).astype(BF16)
        res[base // 4 : base // 4 + 64, :] = mm(own, x_ref[base : base + 256, :])
        for f in range(width // 256):
            nrmt[f * 256 : (f + 1) * 256, base : base + 256] = mm_t(
                eye, nrm[:, f * 256 : (f + 1) * 256]
            ).astype(BF16)

    def forward_qkv(i):
        base = i * 256
        if i == 0:
            load_w.wait()

        def project(c, _):
            at = pl.ds(pl.multiple_of(c * 240, 16), 240)
            qkvt[at, base : base + 256] = mm_t(wt[at, :], nrm[...]).astype(BF16)
            return 0

        lax.fori_loop(0, 3 * hcols // 240, project, 0)

    def forward_attend(i):
        base = i * 256
        live = iota((256, 128), 0) < counts[i]
        cols = pl.ds(base, 256)
        for h in range(heads):
            row = h * 3 * HEAD_V
            k = mm_t(eye, qkvt[row + HEAD_V : row + 2 * HEAD_V, cols]).astype(BF16)
            v_t = qkvt[row + 2 * HEAD_V : row + 3 * HEAD_V, cols]
            for c in range(2):
                lanes = slice(c * 128, (c + 1) * 128)
                q_t = qkvt[row : row + HEAD_V, pl.ds(base + c * 128, 128)]
                scores = mm(k, q_t) * HEAD_V**-0.5
                scores = jnp.where(live, scores, -1e30)
                weights = jnp.exp(scores - jnp.max(scores, axis=0, keepdims=True))
                weights = weights * (1.0 / jnp.sum(weights, axis=0, keepdims=True))
                weights = weights.astype(BF16)
                probs[i * heads + h, :, lanes] = weights
                ot[h * HEAD_V : (h + 1) * HEAD_V, lanes] = mm(v_t, weights).astype(BF16)
        by_patch = ones_where(
            iota((256, 256), 1) == 4 * (iota((256, 256), 0) & 63) + (iota((256, 256), 0) >> 6)
        ).astype(BF16)
        hs[i] = mm_t(by_patch, ot[...]).astype(BF16)

    def send_heads(i):
        out = pl.ds(i * 64, 64)
        for k in to_t:
            heads_in.push(hs.at[i, rows(at_t(k) * 64, 64), :], hm.at[t, out, :], dev_t(k))
        hm[pl.ds(t, 1), out, :] = hs[i, rows(t * 64, 64), :][None]

    row_i, lane_i = iota((256, 256), 0), iota((256, 256), 1)

    def z_to_y():
        return ones_where(
            lane_i == ((row_i >> 3) & (NZ - 1)) * 32 + (row_i >> 6) * 8 + (row_i & 7)
        ).astype(BF16)

    def y_to_g():
        return ones_where(
            lane_i
            == ((row_i >> 5) & (ny - 1)) * 64
            + ((row_i >> 2) & (NZ - 1)) * 8
            + (row_i >> 7) * 4
            + (row_i & 3)
        ).astype(BF16)

    def g_to_z():
        return ones_where(
            lane_i
            == ((row_i >> 2) & 1) * 128
            + ((row_i >> 3) & (ny - 1)) * 32
            + (row_i >> 5) * 4
            + (row_i & 3)
        ).astype(BF16)

    def y_to_z():
        return ones_where(
            lane_i == ((row_i >> 3) & (ny - 1)) * 64 + (row_i >> 5) * 8 + (row_i & 7)
        ).astype(BF16)

    def z_to_g():
        return ones_where(
            lane_i
            == ((row_i >> 2) & (NZ - 1)) * 32
            + ((row_i >> 5) & (ny - 1)) * 8
            + (row_i >> 7) * 4
            + (row_i & 3)
        ).astype(BF16)

    hw = width // 2

    def send_y(buf, dst):
        group = push_all(
            dst.at[pl.ds(0, ny - 1)],
            [(buf.at[rows(at_y(k) * 64, 64), :], dst.at[y], dev_y(k)) for k in (1, 3, 2)],
        )
        dst[pl.ds(y, 1)] = buf[rows(y * 64, 64), :][None]
        return group

    def send_z(buf, dst):
        group = push_all(
            dst.at[pl.ds(0, NZ - 1)],
            [
                (buf.at[rows(at_z(k) * 32, 32), :], dst.at[z], dev_z(k))
                for k in (4, 3, 5, 2, 6, 1, 7)
            ],
        )
        dst[pl.ds(z, 1)] = buf[rows(z * 32, 32), :][None]
        return group

    def send_g(buf, dst):
        group = push_all(
            dst.at[0], [(buf.at[rows((1 - g) * 128, 128), :], dst.at[g], dev_g)]
        )
        dst[pl.ds(g, 1)] = buf[rows(g * 128, 128), :][None]
        return group

    class Exchange:
        def __init__(self, buf, from_y, from_z, from_g):
            self.buf, self.from_y, self.from_z, self.from_g = buf, from_y, from_z, from_g
            self.group = [None, None]

        def begin(self, order, src):
            for j in range(2):
                if j:
                    order = mm(z_to_y(), order).astype(BF16)
                self.buf[j] = mm(order, src[:, j * hw : (j + 1) * hw]).astype(BF16)
                send, to = ((send_z, self.from_z), (send_y, self.from_y))[j]
                self.group[j] = send(self.buf.at[j], to.at[j])

        def next(self, j, came, order, send, to):
            self.group[j].arrived()
            self.group[j].sent()
            self.buf[j] = mm(order(), came[j].reshape(256, hw)).astype(BF16)
            self.group[j] = send(self.buf.at[j], to.at[j])

        def second(self, j):
            if j == 0:
                self.next(0, self.from_z, z_to_y, send_y, self.from_y)
            else:
                self.next(1, self.from_y, y_to_z, send_z, self.from_z)

        def third(self, j):
            if j == 0:
                self.next(0, self.from_y, y_to_g, send_g, self.from_g)
            else:
                self.next(1, self.from_z, z_to_g, send_g, self.from_g)

        def end(self, order, dst):
            for j in range(2):
                self.group[j].arrived()
                dst[:, j * hw : (j + 1) * hw] = mm(
                    order, self.from_g[j].reshape(256, hw)
                ).astype(BF16)

    forward_norm(0)
    forward_qkv(0)
    forward_attend(0)

    pair = iota((256, 128), 0)
    block_lane = iota((256, 128), 1)
    target = jnp.broadcast_to(bt_row, (256, 128)).astype(F32)
    target_of = jnp.sum(jnp.where(block_lane == (pair >> 1), target, 0.0), axis=1, keepdims=True)
    target_of = target_of.astype(I32)
    shard_of = target_of >> 7
    earlier = ((jnp.broadcast_to(bt_row, (256, 128)) >> 7) == shard_of) & (block_lane < (pair >> 1))
    rank_of = jnp.sum(ones_where(earlier), axis=1, keepdims=True).astype(I32)
    row_of = rank_of * 2 + (iota((256, 1), 0) & 1)
    s_g, s_y, s_z = shard_of >> 5, (shard_of >> 3) & (ny - 1), shard_of & (NZ - 1)
    placing[0] = ones_where(lane_i == shard_of * 4 + row_of).astype(BF16)
    to_at = (s_z * 32 + s_y * 8 + s_g * 4 + row_of).astype(F32)
    to_row = jnp.sum(jnp.where(row_i == lane_i, to_at, 0.0), axis=0, keepdims=True).astype(I32)
    placing[1] = ones_where(row_i == to_row).astype(BF16)

    pl.semaphore_wait(barrier, len(partners))

    slots_y = push_all(
        bty.at[pl.ds(0, ny - 1)], [(bts, bty.at[y], dev_y(k)) for k in range(1, ny)]
    )
    weight_part = wf.at[pl.ds(0, nt - 1), pl.ds(0, hrows), :]
    weight_t = push_all(
        weight_part,
        [(ow_hbm.at[own_half, :], wf.at[t, own_half, :], dev_t(k)) for k in to_t],
    )
    heads_in = Group(hm.at[pl.ds(0, nt - 1)])
    send_heads(0)
    bty[pl.ds(y, 1)] = bts[...][None]

    forward_norm(1)
    slots_y.arrived()
    slots_z = push_all(
        btz.at[pl.ds(0, NZ - 1)], [(bty, btz.at[z], dev_z(k)) for k in range(1, NZ)]
    )
    btz[pl.ds(z, 1)] = bty[...][None]
    forward_qkv(1)
    slots_z.arrived()
    slots_g = push_all(btg.at[0], [(btz, btg.at[g], dev_g)])
    btg[pl.ds(g, 1)] = btz[...][None]
    load_c.wait()
    slots_g.arrived()
    lanes3 = (ny * NZ, 8, 128)
    sub3 = iota(lanes3, 1)
    both = jnp.where(sub3 < 4, btg[0].reshape(lanes3), btg[1].reshape(lanes3))
    hit = (both >> 7) == (g * ny * NZ + s)
    slot = (both & 127).astype(F32)
    lane3 = iota(lanes3, 2).astype(F32)
    first_lane = jnp.min(jnp.where(hit, lane3, 999.0), axis=2, keepdims=True)
    slot_0 = jnp.sum(jnp.where(hit & (lane3 == first_lane), slot, 0.0), axis=2, keepdims=True)
    slot_1 = jnp.sum(jnp.where(hit & (lane3 != first_lane), slot, 0.0), axis=2, keepdims=True)
    sub1 = iota((ny * NZ, 8, 1), 1)
    slot_row = jnp.where((sub1 & 2) == 2, slot_1, slot_0) * 2.0 + (sub1 & 1).astype(F32)
    slot_row = slot_row.reshape(256, 1)
    cot = Exchange(cs, cyr, czr, cgr)
    cot.begin(ones_where(lane_i.astype(F32) == slot_row).astype(BF16), cot_ref)
    slot_lane = jnp.sum(jnp.where(row_i == lane_i, slot_row, 0.0), axis=0, keepdims=True)
    back_at = ones_where(row_i.astype(F32) == slot_lane).astype(BF16)
    returning[...] = mm(back_at, g_to_z()).astype(BF16)

    forward_attend(1)
    send_heads(1)
    forward_norm(2)
    forward_qkv(2)
    cot.second(1)
    forward_attend(2)
    send_heads(2)
    forward_norm(3)
    forward_qkv(3)
    cot.second(0)
    forward_attend(3)
    send_heads(3)
    weight_t.arrived()
    weight_g = push_all(
        weight_part,
        [
            (wf.at[at_t(nt - k), own_half, :], wf.at[at_t(nt - k), own_half, :], dev_g)
            for k in to_t
        ],
    )
    load_o.wait()
    cot.third(0)
    heads_in.arrived()
    wide = hcols - 128
    for q in range(nt):
        hmt[q] = mm_t(eye[:wide, :wide], hm[q, :, 128:]).astype(BF16)
    cot.third(1)
    weight_g.arrived()

    def project_out(c, _):
        cols = pl.ds(pl.multiple_of(c * 256, 256), 256)
        total = res[:, cols]
        for q in range(nt):
            total += mm(hm[q], wf[q, :, cols])
        res[:, cols] = total
        return 0

    lax.fori_loop(0, width // 256, project_out, 0)
    cot.end(placing[0], inc)

    def merge_rows(c, _):
        at = pl.ds(pl.multiple_of(c * 32, 32), 32)
        center, scale = norm_parts(res[at, :])
        hat = center * scale
        alive = ones_where(4 * ((iota((32, 1), 0) + c * 32) & 63) < counts[lax.div(c, 2)])
        merged[at, :] = (hat * gain_m * alive).astype(BF16)
        grad = inc[at, :].astype(F32) * alive * gain_m
        mean_grad = jnp.mean(grad, axis=-1, keepdims=True)
        mean_hat = jnp.mean(grad * hat, axis=-1, keepdims=True)
        gown[at, :] = (scale * (grad - mean_grad - hat * mean_hat)).astype(BF16)
        return 0

    lax.fori_loop(0, 8, merge_rows, 0, unroll=2)

    pairs = 2
    prows = hcols // pairs
    grads_in = [Group(ghr.at[pl.ds(0, nt - 1), pl.ds(0, prows), :]) for _ in range(pairs)]

    def grads_for(k):
        q = at_t(k)
        ghs[pl.ds(q, 1)] = mm_t(wf[pl.ds(q, 1)].reshape(hcols, width), gown[...]).astype(BF16)[None]

    def send_grads(j, k):
        part = pl.ds(j * prows, prows)
        grads_in[j].push(ghs.at[at_t(k), part, :], ghr.at[t, part, :], dev_t(k))

    for k in to_t:
        grads_for(k)
        send_grads(0, k)
    for k in to_t:
        send_grads(1, k)
    grads_for(0)
    ghr[pl.ds(t, 1)] = ghs[pl.ds(t, 1)]

    row = Exchange(ms, myr, mzr, mgr)
    row.begin(placing[1], merged)

    for f in range(width // 256):
        gownt[f * 256 : (f + 1) * 256, :] = mm_t(eye, gown[:, f * 256 : (f + 1) * 256]).astype(BF16)
    def terms_b(side):
        def one(c, _):
            at = pl.ds(pl.multiple_of(side * half + c * (half // 2), 64), half // 2)
            to = pl.ds(pl.multiple_of(c * (half // 2), 64), half // 2)
            for q in range(nt):
                ob[pl.ds(side, 1), to, q * 128 : (q + 1) * 128] = mm(
                    gownt[at, :], hm[q, :, :128]
                ).astype(BF16)[None]
            return 0

        lax.fori_loop(0, 2, one, 0)

    def terms_a(side, k):
        cols = pl.ds(pl.multiple_of(side * half, 128), half)
        q = at_t(k)
        value = mm(hmt[pl.ds(q, 1)].reshape(wide, 256), gown[:, cols])
        oa[pl.ds(side, 1), pl.ds(q, 1)] = value.astype(BF16)[None, None]

    terms_b(1 - g)
    b = push_all(obg, [(ob.at[1 - g], obg, dev_g)])
    a = []
    for k in to_t + (0,):
        terms_a(1 - g, k)
        a.append(push_all(oag.at[0], [(oa.at[1 - g, at_t(k)], oag.at[at_t(k)], dev_g)]))
    terms_b(g)

    def spread(j):
        def one(i, _):
            cols = pl.ds(pl.multiple_of(i * 256, 256), 256)
            total = jnp.zeros((prows, 256), F32)
            for p in range(nt):
                order = ones_where(lane_i == 4 * (row_i - 64 * i) + p).astype(BF16)
                total += mm(ghr[p, j * prows : (j + 1) * prows, :], order)
            ght[j * prows : (j + 1) * prows, cols] = total.astype(BF16)
            return 0

        lax.fori_loop(0, images, one, 0)

    def back_head(h):
        row = h * 3 * HEAD_V

        def back_image(i, _):
            cols = pl.ds(pl.multiple_of(i * 256, 256), 256)
            at_q, at_k, at_v = row, row + HEAD_V, row + 2 * HEAD_V
            q_t = qkvt[at_q : at_q + HEAD_V, cols]
            k_t = qkvt[at_k : at_k + HEAD_V, cols]
            v_t = qkvt[at_v : at_v + HEAD_V, cols]
            d_t = ght[h * HEAD_V : (h + 1) * HEAD_V, cols]
            v = mm_t(eye, v_t).astype(BF16)
            weights = probs[i * heads + h]
            grad_v = mm_t(d_t, weights).astype(BF16)
            parts = []
            for c in range(2):
                lanes = slice(c * 128, (c + 1) * 128)
                w = weights[:, lanes].astype(F32)
                grad_w = mm(v, d_t[:, lanes]).astype(BF16).astype(F32)
                inner = jnp.sum(w * grad_w, axis=0, keepdims=True)
                parts.append((w * (grad_w - inner) * HEAD_V**-0.5).astype(BF16))
            grad_s = jnp.concatenate(parts, axis=1)
            grad_q = mm(k_t, grad_s).astype(BF16)
            grad_k = mm_t(q_t, grad_s).astype(BF16)
            qkvt[at_q : at_q + HEAD_V, cols] = grad_q
            qkvt[at_k : at_k + HEAD_V, cols] = grad_k
            qkvt[at_v : at_v + HEAD_V, cols] = grad_v
            return 0

        lax.fori_loop(0, images, back_image, 0, unroll=4)

    def weight_terms(h, side):
        def one(c, _):
            at = pl.ds(pl.multiple_of(side * half + c * (half // 2), 64), half // 2)
            dws[h, at, :] = mm_t(
                nrmt[at, :], qkvt[h * 3 * HEAD_V : (h + 1) * 3 * HEAD_V, :]
            ).astype(BF16)
            return 0

        lax.fori_loop(0, 2, one, 0)

    def to_shards():
        r, c = iota((NZ * 32, yrows), 0), iota((NZ * 32, yrows), 1)
        return ones_where((c == (r >> 5) * zrows + (r & 31)) & ((r & 31) < zrows)).astype(BF16)

    def add(a, b):
        return a.astype(F32) + b.astype(F32)

    their_rows = pl.ds(pl.multiple_of((1 - g) * half, 128), half)
    own_rows = pl.ds(pl.multiple_of(g * half, 128), half)
    order_y = [(k, k - 1) for k in (1, 3, 2)]
    order_z = [(k, k - 1) for k in (4, 3, 5, 2, 6, 1, 7)]

    def rows_y(k):
        return pl.ds(pl.multiple_of(at_y(k) * yrows, 16), yrows)

    def weight_start(h):
        weight_terms(h, 1 - g)
        group = push_all(dgr.at[h], [(dws.at[h, their_rows, :], dgr.at[h], dev_g)])
        weight_terms(h, g)
        return group

    def weight_y(h, group):
        group.arrived()
        dgr[h] = add(dws[h, own_rows, :], dgr[h]).astype(BF16)
        return push_all(
            dyr.at[h], [(dgr.at[h, rows_y(k), :], dyr.at[h, j], dev_y(k)) for k, j in order_y]
        )

    def weight_z(h, group):
        group.arrived()
        total = dgr[h, rows_y(0), :].astype(F32)
        for k in range(1, ny):
            total += dyr[h, k - 1].astype(F32)
        dz[h] = mm(to_shards(), total.astype(BF16)).astype(BF16)
        return push_all(
            dzr.at[h],
            [(dz.at[h, rows(at_z(k) * 32, 32), :], dzr.at[h, j], dev_z(k)) for k, j in order_z],
        )

    def weight_end(h, group):
        group.arrived()
        total = dz[h, rows(z * 32, 32), :].astype(F32)
        for k in range(1, NZ):
            total += dzr[h, k - 1].astype(F32)
        gq_ref[:, h * 3 * HEAD_V : (h + 1) * 3 * HEAD_V] = total[:zrows]

    def b_y(group):
        group.arrived()
        obg[...] = add(ob[pl.ds(g, 1)].reshape(half, nt * 128), obg[...]).astype(BF16)
        return push_all(obyr, [(obg.at[rows_y(k), :], obyr.at[j], dev_y(k)) for k, j in order_y])

    def b_x(group):
        group.arrived()
        total = obg[rows_y(0), :].astype(F32)
        for k in range(1, ny):
            total += obyr[k - 1].astype(F32)
        for q in range(nt):
            obx[q] = total[:, q * 128 : (q + 1) * 128].astype(BF16)
        return push_all(obxr, [(obx.at[at_t(k)], obxr.at[k - 1], dev_t(k)) for k in to_t])

    def b_z(group):
        group.arrived()
        total = obx[pl.ds(t, 1)].reshape(yrows, 128).astype(F32)
        for k in range(1, nt):
            total += obxr[k - 1].astype(F32)
        obz[...] = mm(to_shards(), total.astype(BF16)).astype(BF16)
        return push_all(
            obzr, [(obz.at[rows(at_z(k) * 32, 32), :], obzr.at[j], dev_z(k)) for k, j in order_z]
        )

    def b_end(group):
        group.arrived()
        total = obz[rows(z * 32, 32), :].astype(F32)
        for k in range(1, NZ):
            total += obzr[k - 1].astype(F32)
        go_ref[:, :128] = total[:zrows]

    def a_x(groups):
        out = Group(oax)
        for k, group in zip(to_t + (0,), groups):
            group.arrived()
            q = at_t(k)
            mine = oa[pl.ds(g, 1), pl.ds(q, 1)].reshape(wide, half)
            oag[pl.ds(q, 1)] = add(mine, oag[pl.ds(q, 1)].reshape(wide, half)).astype(BF16)[None]
            if k:
                out.push(oag.at[q], oax.at[k - 1], dev_t(k))
        return out

    def a_y(group):
        group.arrived()
        for f in range(half // 128):
            cols = slice(f * 128, (f + 1) * 128)
            total = oag[pl.ds(t, 1), :, cols].reshape(wide, 128).astype(F32)
            for k in range(1, nt):
                total += oax[k - 1, :, cols].astype(F32)
            oay[cols, :] = mm_t(eye[:128, :128], total.astype(BF16)).astype(BF16)
        return push_all(oayr, [(oay.at[rows_y(k), :], oayr.at[j], dev_y(k)) for k, j in order_y])

    def a_z(group):
        group.arrived()
        total = oay[rows_y(0), :].astype(F32)
        for k in range(1, ny):
            total += oayr[k - 1].astype(F32)
        oaz[...] = mm(to_shards(), total.astype(BF16)).astype(BF16)
        return push_all(
            oazr, [(oaz.at[rows(at_z(k) * 32, 32), :], oazr.at[j], dev_z(k)) for k, j in order_z]
        )

    def a_end(group):
        group.arrived()
        total = oaz[rows(z * 32, 32), :].astype(F32)
        for k in range(1, NZ):
            total += oazr[k - 1].astype(F32)
        go_ref[:, 128:] = total[:zrows]

    b = b_y(b)
    for k in to_t + (0,):
        terms_a(g, k)
    grads_in[0].arrived()
    spread(0)
    back_head(0)
    a = a_x(a)
    w0 = weight_start(0)
    row.second(1)
    back_head(1)
    w0 = weight_y(0, w0)
    row.second(0)
    w1 = weight_start(1)
    grads_in[1].arrived()
    spread(1)
    b = b_x(b)
    back_head(2)
    w1 = weight_y(1, w1)
    w2 = weight_start(2)
    w0 = weight_z(0, w0)
    b = b_z(b)
    a = a_y(a)
    back_head(3)
    w2 = weight_y(2, w2)
    w1 = weight_z(1, w1)
    w3 = weight_start(3)
    row.third(0)
    a = a_z(a)
    w3 = weight_y(3, w3)
    row.third(1)
    w2 = weight_z(2, w2)
    weight_end(0, w0)
    b_end(b)
    weight_end(1, w1)
    w3 = weight_z(3, w3)
    row.end(returning[...], image)
    store_i = pltpu.make_async_copy(image, image_hbm, lsem.at[images + 3])
    store_i.start()
    a_end(a)
    weight_end(2, w2)
    weight_end(3, w3)
    store_i.wait()
    for group in list(open_sends.values()):
        group.sent()
    assert used[0] == n_sems


def hand_over(a, b, c, a_out, b_out, c_out):
    a_out[...] = a[...]
    b_out[...] = b[...]
    c_out[...] = c[...]


def shards(
    ny, nt, patches_in, gain_attn, gain_merge, qkv_weight, out_weight, cotangent, patch_counts, block_target
):
    row_count, width = patches_in.shape
    images = patch_counts.shape[0]
    hcols = out_weight.shape[0]
    heads = hcols // HEAD_V
    cols = 3 * HEAD_V
    half, yrows = width // 2, width // 2 // ny
    wide = hcols - 128
    zrows = yrows // NZ
    n_sems = 3 + 2 + 1 + 6 + 6 + 2 + 4 + (nt + 3) + 3 * heads
    v = pltpu.VMEM
    scratch = [
        v((row_count, width), BF16),
        v((3 * hcols, width), BF16),
        v((256, width), BF16),
        v((256, width), BF16),
        v((width, row_count), BF16),
        v((3 * hcols, row_count), BF16),
        v((images * heads, 256, 256), BF16),
        v((hcols, 256), BF16),
        v((images, 256, hcols), BF16),
        v((nt, 256, hcols), BF16),
        v((nt, hcols, width), BF16),
        v((256, width), F32),
        v((8, 128), I32),
        v((ny, 8, 128), I32),
        v((NZ, ny, 8, 128), I32),
        v((2, NZ, ny, 8, 128), I32),
        v((2, 256, 256), BF16),
        v((256, 256), BF16),
        v((2, 256, half), BF16),
        v((2, ny, 64, half), BF16),
        v((2, NZ, 32, half), BF16),
        v((2, 2, 128, half), BF16),
        v((2, 256, half), BF16),
        v((2, ny, 64, half), BF16),
        v((2, NZ, 32, half), BF16),
        v((2, 2, 128, half), BF16),
        v((256, width), BF16),
        v((256, width), BF16),
        v((256, width), BF16),
        v((256, width), BF16),
        v((width, 256), BF16),
        v((nt, wide, 256), BF16),
        v((nt, hcols, 256), BF16),
        v((nt, hcols, 256), BF16),
        v((hcols, row_count), BF16),
        v((2, nt, wide, half), BF16),
        v((nt, wide, half), BF16),
        v((nt - 1, wide, half), BF16),
        v((half, wide), BF16),
        v((ny - 1, yrows, wide), BF16),
        v((NZ * 32, wide), BF16),
        v((NZ - 1, 32, wide), BF16),
        v((2, half, nt * 128), BF16),
        v((half, nt * 128), BF16),
        v((ny - 1, yrows, nt * 128), BF16),
        v((nt, yrows, 128), BF16),
        v((nt - 1, yrows, 128), BF16),
        v((NZ * 32, 128), BF16),
        v((NZ - 1, 32, 128), BF16),
        v((heads, width, cols), BF16),
        v((heads, half, cols), BF16),
        v((heads, ny - 1, yrows, cols), BF16),
        v((heads, NZ * 32, cols), BF16),
        v((heads, NZ - 1, 32, cols), BF16),
        pltpu.SemaphoreType.DMA((images + 4,)),
        pltpu.SemaphoreType.DMA((n_sems,)),
        pltpu.SemaphoreType.DMA((n_sems,)),
    ]
    in_vmem = pl.BlockSpec(memory_space=pltpu.VMEM)
    in_hbm = pl.BlockSpec(memory_space=pl.ANY)
    image_rows, gq, go = pl.pallas_call(
        functools.partial(kernel, ny, nt, n_sems),
        out_shape=(
            jax.ShapeDtypeStruct((256, width), BF16),
            jax.ShapeDtypeStruct((zrows, heads * cols), F32),
            jax.ShapeDtypeStruct((zrows, hcols), F32),
        ),
        in_specs=[pl.BlockSpec(memory_space=pltpu.SMEM)] + [in_vmem] * 3 + [in_hbm] * 4,
        out_specs=(in_hbm, in_vmem, in_vmem),
        scratch_shapes=scratch,
        compiler_params=pltpu.CompilerParams(
            collective_id=0, has_side_effects=True, vmem_limit_bytes=62 << 20
        ),
        name="block",
    )(
        patch_counts,
        gain_attn,
        gain_merge,
        block_target.reshape(1, -1),
        patches_in,
        qkv_weight.T,
        out_weight,
        cotangent,
    )
    image_rows, grad_qkv, grad_out = pl.pallas_call(
        hand_over,
        out_shape=tuple(jax.ShapeDtypeStruct(a.shape, a.dtype) for a in (image_rows, gq, go)),
        in_specs=[in_vmem] * 3,
        out_specs=(in_vmem,) * 3,
        name="hand_over",
    )(image_rows, gq, go)
    return image_rows, grad_qkv, grad_out.T


def solution(mesh):
    ny, nt = mesh.shape["seq"] // NZ, mesh.shape["tp"]
    return jax.shard_map(
        functools.partial(shards, ny, nt),
        mesh=mesh,
        in_specs=(
            P(("grp", "seq"), None),
            P(),
            P(),
            P(None, "tp"),
            P("tp", None),
            P(("grp", "seq"), "tp"),
            P(("grp", "seq")),
            P(("grp", "seq")),
        ),
        out_specs=(P(("grp", "seq"), "tp"), P(("grp", "seq"), "tp"), P("tp", ("grp", "seq"))),
        check_vma=False,
    )
```

```python
import functools

import jax
import jax.numpy as jnp
from jax import lax
from jax.experimental import pallas as pl
from jax.experimental.pallas import tpu as pltpu
from jax.sharding import PartitionSpec as P

HEAD_V = 80
NZ = 8
F32 = jnp.float32
BF16 = jnp.bfloat16
I32 = jnp.int32
MESH = pl.DeviceIdType.MESH


def mm(a, b):
    return lax.dot_general(a, b, (((1,), (0,)), ((), ())), preferred_element_type=F32)


def mm_t(a, b):
    return lax.dot_general(a, b, (((1,), (1,)), ((), ())), preferred_element_type=F32)


def iota(shape, dim):
    return lax.broadcasted_iota(I32, shape, dim)


def ones_where(cond):
    return jnp.where(cond, 1.0, 0.0)


def norm_parts(values):
    center = values - jnp.mean(values, axis=-1, keepdims=True)
    spread = jnp.mean(center * center, axis=-1, keepdims=True)
    return center, lax.rsqrt(spread + 1e-06)


def kernel(
    ny,
    nt,
    n_sems,
    counts,
    ga_ref,
    gm_ref,
    bt_ref,
    x_hbm,
    wt_hbm,
    ow_hbm,
    cot_hbm,
    image_hbm,
    gq_ref,
    go_ref,
    x_ref,
    wt,
    cot_ref,
    nrm,
    nrmt,
    qkvt,
    probs,
    ot,
    hs,
    hm,
    wf,
    res,
    bts,
    bty,
    btz,
    btg,
    placing,
    returning,
    cs,
    cyr,
    czr,
    cgr,
    ms,
    myr,
    mzr,
    mgr,
    inc,
    image,
    merged,
    gown,
    gownt,
    hmt,
    ghs,
    ghr,
    ght,
    oa,
    oag,
    oax,
    oay,
    oayr,
    oaz,
    oazr,
    ob,
    obg,
    obyr,
    obx,
    obxr,
    obz,
    obzr,
    dws,
    dgr,
    dyr,
    dz,
    dzr,
    lsem,
    ssem,
    rsem,
):
    g = lax.axis_index("grp")
    s = lax.axis_index("seq")
    t = lax.axis_index("tp")
    y = lax.div(s, NZ)
    z = lax.rem(s, NZ)
    images = x_ref.shape[0] // 256
    width = x_ref.shape[1]
    hcols = wt.shape[0] // 3
    heads = hcols // HEAD_V
    half = width // 2
    yrows = half // ny
    zrows = yrows // NZ

    def at_z(k):
        return lax.rem(z + k, NZ)

    def at_y(k):
        return lax.rem(y + k, ny)

    def at_t(k):
        return lax.rem(t + k, nt)

    def dev_z(k):
        return {"seq": y * NZ + at_z(k)}

    def dev_y(k):
        return {"seq": at_y(k) * NZ + z}

    def dev_t(k):
        return {"tp": at_t(k)}

    dev_g = {"grp": 1 - g}
    to_t = (1, 3, 2)

    used = [0]
    open_sends = {}

    class Group:
        def __init__(self, whole):
            self.k = used[0]
            used[0] += 1
            self.whole = self.copy(whole, whole, dev_g)
            open_sends[self.k] = self

        def copy(self, src, dst, device):
            return pltpu.make_async_remote_copy(
                src_ref=src,
                dst_ref=dst,
                send_sem=ssem.at[self.k],
                recv_sem=rsem.at[self.k],
                device_id=device,
                device_id_type=MESH,
            )

        def push(self, src, dst, device):
            self.copy(src, dst, device).start()
            return self

        def arrived(self):
            self.whole.wait_recv()

        def sent(self):
            self.whole.wait_send()
            del open_sends[self.k]

    def push_all(whole, pieces):
        group = Group(whole)
        for piece in pieces:
            group.push(*piece)
        return group

    def rows(start, size):
        return pl.ds(pl.multiple_of(start, size if size & (size - 1) == 0 else 16), size)

    barrier = pltpu.get_barrier_semaphore()
    partners = (
        [dev_z(k) for k in range(1, NZ)]
        + [dev_y(k) for k in range(1, ny)]
        + [dev_t(k) for k in range(1, nt)]
        + [dev_g]
    )
    for device in partners:
        pl.semaphore_signal(barrier, inc=1, device_id=device, device_id_type=MESH)

    def image_rows_of(i):
        at = pl.ds(i * 256, 256)
        return pltpu.make_async_copy(x_hbm.at[at, :], x_ref.at[at, :], lsem.at[i])

    loads_x = [image_rows_of(i) for i in range(images)]
    load_w = pltpu.make_async_copy(wt_hbm, wt, lsem.at[images])
    load_c = pltpu.make_async_copy(cot_hbm, cot_ref, lsem.at[images + 1])
    load_o = pltpu.make_async_copy(ow_hbm, wf.at[t], lsem.at[images + 2])
    loads_x[0].start()
    load_w.start()
    load_c.start()

    for load in loads_x[1:]:
        load.start()
    load_o.start()
    hrows = hcols // 2
    own_half = pl.ds(pl.multiple_of(g * hrows, 16), hrows)
    eye = ones_where(iota((256, 256), 0) == iota((256, 256), 1)).astype(BF16)
    bt_row = bt_ref[...]
    bts[...] = jnp.broadcast_to(bt_row, bts.shape)
    gain_a = ga_ref[...].reshape(1, width)
    gain_m = gm_ref[...].reshape(1, width)

    def forward_norm(i):
        base = i * 256
        loads_x[i].wait()

        def norm_rows(c, _):
            at = pl.ds(pl.multiple_of(c * 32, 32), 32)
            values = x_ref[pl.ds(pl.multiple_of(base + c * 32, 32), 32), :].astype(F32)
            center, scale = norm_parts(values)
            nrm[at, :] = (center * scale * gain_a).astype(BF16)
            return 0

        lax.fori_loop(0, 8, norm_rows, 0, unroll=4)
        own = ones_where(iota((64, 256), 1) == 4 * iota((64, 256), 0) + t).astype(BF16)
        res[base // 4 : base // 4 + 64, :] = mm(own, x_ref[base : base + 256, :])
        for f in range(width // 256):
            nrmt[f * 256 : (f + 1) * 256, base : base + 256] = mm_t(
                eye, nrm[:, f * 256 : (f + 1) * 256]
            ).astype(BF16)

    def forward_qkv(i):
        base = i * 256
        if i == 0:
            load_w.wait()

        def project(c, _):
            at = pl.ds(pl.multiple_of(c * 240, 16), 240)
            qkvt[at, base : base + 256] = mm_t(wt[at, :], nrm[...]).astype(BF16)
            return 0

        lax.fori_loop(0, 3 * hcols // 240, project, 0, unroll=2)

    def forward_attend(i):
        base = i * 256
        live = iota((256, 128), 0) < counts[i]
        cols = pl.ds(base, 256)
        for h in range(heads):
            row = h * 3 * HEAD_V
            k = mm_t(eye, qkvt[row + HEAD_V : row + 2 * HEAD_V, cols]).astype(BF16)
            v_t = qkvt[row + 2 * HEAD_V : row + 3 * HEAD_V, cols]
            for c in range(2):
                lanes = slice(c * 128, (c + 1) * 128)
                q_t = qkvt[row : row + HEAD_V, pl.ds(base + c * 128, 128)]
                scores = mm(k, q_t) * HEAD_V**-0.5
                scores = jnp.where(live, scores, -1e30)
                weights = jnp.exp(scores - jnp.max(scores, axis=0, keepdims=True))
                weights = weights * (1.0 / jnp.sum(weights, axis=0, keepdims=True))
                weights = weights.astype(BF16)
                probs[i * heads + h, :, lanes] = weights
                ot[h * HEAD_V : (h + 1) * HEAD_V, lanes] = mm(v_t, weights).astype(BF16)
        by_patch = ones_where(
            iota((256, 256), 1) == 4 * (iota((256, 256), 0) & 63) + (iota((256, 256), 0) >> 6)
        ).astype(BF16)
        hs[i] = mm_t(by_patch, ot[...]).astype(BF16)

    def send_heads(i):
        out = pl.ds(i * 64, 64)
        for k in to_t:
            heads_in.push(hs.at[i, rows(at_t(k) * 64, 64), :], hm.at[t, out, :], dev_t(k))
        hm[pl.ds(t, 1), out, :] = hs[i, rows(t * 64, 64), :][None]

    row_i, lane_i = iota((256, 256), 0), iota((256, 256), 1)

    def z_to_y():
        return ones_where(
            lane_i == ((row_i >> 3) & (NZ - 1)) * 32 + (row_i >> 6) * 8 + (row_i & 7)
        ).astype(BF16)

    def y_to_g():
        return ones_where(
            lane_i
            == ((row_i >> 5) & (ny - 1)) * 64
            + ((row_i >> 2) & (NZ - 1)) * 8
            + (row_i >> 7) * 4
            + (row_i & 3)
        ).astype(BF16)

    def g_to_z():
        return ones_where(
            lane_i
            == ((row_i >> 2) & 1) * 128
            + ((row_i >> 3) & (ny - 1)) * 32
            + (row_i >> 5) * 4
            + (row_i & 3)
        ).astype(BF16)

    def y_to_z():
        return ones_where(
            lane_i == ((row_i >> 3) & (ny - 1)) * 64 + (row_i >> 5) * 8 + (row_i & 7)
        ).astype(BF16)

    def z_to_g():
        return ones_where(
            lane_i
            == ((row_i >> 2) & (NZ - 1)) * 32
            + ((row_i >> 5) & (ny - 1)) * 8
            + (row_i >> 7) * 4
            + (row_i & 3)
        ).astype(BF16)

    hw = width // 2

    def send_y(buf, dst):
        group = push_all(
            dst.at[pl.ds(0, ny - 1)],
            [(buf.at[rows(at_y(k) * 64, 64), :], dst.at[y], dev_y(k)) for k in (1, 3, 2)],
        )
        dst[pl.ds(y, 1)] = buf[rows(y * 64, 64), :][None]
        return group

    def send_z(buf, dst):
        group = push_all(
            dst.at[pl.ds(0, NZ - 1)],
            [
                (buf.at[rows(at_z(k) * 32, 32), :], dst.at[z], dev_z(k))
                for k in (4, 3, 5, 2, 6, 1, 7)
            ],
        )
        dst[pl.ds(z, 1)] = buf[rows(z * 32, 32), :][None]
        return group

    def send_g(buf, dst):
        group = push_all(
            dst.at[0], [(buf.at[rows((1 - g) * 128, 128), :], dst.at[g], dev_g)]
        )
        dst[pl.ds(g, 1)] = buf[rows(g * 128, 128), :][None]
        return group

    class Exchange:
        def __init__(self, buf, from_y, from_z, from_g):
            self.buf, self.from_y, self.from_z, self.from_g = buf, from_y, from_z, from_g
            self.group = [None, None]

        def begin(self, order, src):
            for j in range(2):
                if j:
                    order = mm(z_to_y(), order).astype(BF16)
                self.buf[j] = mm(order, src[:, j * hw : (j + 1) * hw]).astype(BF16)
                send, to = ((send_z, self.from_z), (send_y, self.from_y))[j]
                self.group[j] = send(self.buf.at[j], to.at[j])

        def next(self, j, came, order, send, to):
            self.group[j].arrived()
            self.group[j].sent()
            self.buf[j] = mm(order(), came[j].reshape(256, hw)).astype(BF16)
            self.group[j] = send(self.buf.at[j], to.at[j])

        def second(self, j):
            if j == 0:
                self.next(0, self.from_z, z_to_y, send_y, self.from_y)
            else:
                self.next(1, self.from_y, y_to_z, send_z, self.from_z)

        def third(self, j):
            if j == 0:
                self.next(0, self.from_y, y_to_g, send_g, self.from_g)
            else:
                self.next(1, self.from_z, z_to_g, send_g, self.from_g)

        def end(self, order, dst):
            for j in range(2):
                self.group[j].arrived()
                dst[:, j * hw : (j + 1) * hw] = mm(
                    order, self.from_g[j].reshape(256, hw)
                ).astype(BF16)

    forward_norm(0)
    forward_qkv(0)
    forward_attend(0)

    pair = iota((256, 128), 0)
    block_lane = iota((256, 128), 1)
    target = jnp.broadcast_to(bt_row, (256, 128)).astype(F32)
    target_of = jnp.sum(jnp.where(block_lane == (pair >> 1), target, 0.0), axis=1, keepdims=True)
    target_of = target_of.astype(I32)
    shard_of = target_of >> 7
    earlier = ((jnp.broadcast_to(bt_row, (256, 128)) >> 7) == shard_of) & (block_lane < (pair >> 1))
    rank_of = jnp.sum(ones_where(earlier), axis=1, keepdims=True).astype(I32)
    row_of = rank_of * 2 + (iota((256, 1), 0) & 1)
    s_g, s_y, s_z = shard_of >> 5, (shard_of >> 3) & (ny - 1), shard_of & (NZ - 1)
    placing[0] = ones_where(lane_i == shard_of * 4 + row_of).astype(BF16)
    to_at = (s_z * 32 + s_y * 8 + s_g * 4 + row_of).astype(F32)
    to_row = jnp.sum(jnp.where(row_i == lane_i, to_at, 0.0), axis=0, keepdims=True).astype(I32)
    placing[1] = ones_where(row_i == to_row).astype(BF16)

    pl.semaphore_wait(barrier, len(partners))

    slots_y = push_all(
        bty.at[pl.ds(0, ny - 1)], [(bts, bty.at[y], dev_y(k)) for k in range(1, ny)]
    )
    weight_part = wf.at[pl.ds(0, nt - 1), pl.ds(0, hrows), :]
    weight_t = push_all(
        weight_part,
        [(ow_hbm.at[own_half, :], wf.at[t, own_half, :], dev_t(k)) for k in to_t],
    )
    heads_in = Group(hm.at[pl.ds(0, nt - 1)])
    send_heads(0)
    bty[pl.ds(y, 1)] = bts[...][None]

    forward_norm(1)
    slots_y.arrived()
    slots_z = push_all(
        btz.at[pl.ds(0, NZ - 1)], [(bty, btz.at[z], dev_z(k)) for k in range(1, NZ)]
    )
    btz[pl.ds(z, 1)] = bty[...][None]
    forward_qkv(1)
    slots_z.arrived()
    slots_g = push_all(btg.at[0], [(btz, btg.at[g], dev_g)])
    btg[pl.ds(g, 1)] = btz[...][None]
    load_c.wait()
    slots_g.arrived()
    lanes3 = (ny * NZ, 8, 128)
    sub3 = iota(lanes3, 1)
    both = jnp.where(sub3 < 4, btg[0].reshape(lanes3), btg[1].reshape(lanes3))
    hit = (both >> 7) == (g * ny * NZ + s)
    slot = (both & 127).astype(F32)
    lane3 = iota(lanes3, 2).astype(F32)
    first_lane = jnp.min(jnp.where(hit, lane3, 999.0), axis=2, keepdims=True)
    slot_0 = jnp.sum(jnp.where(hit & (lane3 == first_lane), slot, 0.0), axis=2, keepdims=True)
    slot_1 = jnp.sum(jnp.where(hit & (lane3 != first_lane), slot, 0.0), axis=2, keepdims=True)
    sub1 = iota((ny * NZ, 8, 1), 1)
    slot_row = jnp.where((sub1 & 2) == 2, slot_1, slot_0) * 2.0 + (sub1 & 1).astype(F32)
    slot_row = slot_row.reshape(256, 1)
    cot = Exchange(cs, cyr, czr, cgr)
    cot.begin(ones_where(lane_i.astype(F32) == slot_row).astype(BF16), cot_ref)
    slot_lane = jnp.sum(jnp.where(row_i == lane_i, slot_row, 0.0), axis=0, keepdims=True)
    back_at = ones_where(row_i.astype(F32) == slot_lane).astype(BF16)
    returning[...] = mm(back_at, g_to_z()).astype(BF16)

    forward_attend(1)
    send_heads(1)
    forward_norm(2)
    forward_qkv(2)
    cot.second(1)
    forward_attend(2)
    send_heads(2)
    forward_norm(3)
    forward_qkv(3)
    cot.second(0)
    forward_attend(3)
    send_heads(3)
    weight_t.arrived()
    weight_g = push_all(
        weight_part,
        [
            (wf.at[at_t(nt - k), own_half, :], wf.at[at_t(nt - k), own_half, :], dev_g)
            for k in to_t
        ],
    )
    load_o.wait()
    cot.third(0)
    heads_in.arrived()
    wide = hcols - 128
    for q in range(nt):
        hmt[q] = mm_t(eye[:wide, :wide], hm[q, :, 128:]).astype(BF16)
    cot.third(1)
    weight_g.arrived()

    def project_out(c, _):
        cols = pl.ds(pl.multiple_of(c * 256, 256), 256)
        total = res[:, cols]
        for q in range(nt):
            total += mm(hm[q], wf[q, :, cols])
        res[:, cols] = total
        return 0

    lax.fori_loop(0, width // 256, project_out, 0)
    cot.end(placing[0], inc)

    def merge_rows(c, _):
        at = pl.ds(pl.multiple_of(c * 32, 32), 32)
        center, scale = norm_parts(res[at, :])
        hat = center * scale
        alive = ones_where(4 * ((iota((32, 1), 0) + c * 32) & 63) < counts[lax.div(c, 2)])
        merged[at, :] = (hat * gain_m * alive).astype(BF16)
        grad = inc[at, :].astype(F32) * alive * gain_m
        mean_grad = jnp.mean(grad, axis=-1, keepdims=True)
        mean_hat = jnp.mean(grad * hat, axis=-1, keepdims=True)
        gown[at, :] = (scale * (grad - mean_grad - hat * mean_hat)).astype(BF16)
        return 0

    lax.fori_loop(0, 8, merge_rows, 0, unroll=4)

    pairs = 2
    prows = hcols // pairs
    grads_in = [Group(ghr.at[pl.ds(0, nt - 1), pl.ds(0, prows), :]) for _ in range(pairs)]

    def grads_for(k):
        q = at_t(k)
        ghs[pl.ds(q, 1)] = mm_t(wf[pl.ds(q, 1)].reshape(hcols, width), gown[...]).astype(BF16)[None]

    def send_grads(j, k):
        part = pl.ds(j * prows, prows)
        grads_in[j].push(ghs.at[at_t(k), part, :], ghr.at[t, part, :], dev_t(k))

    for k in to_t:
        grads_for(k)
        send_grads(0, k)
    for k in to_t:
        send_grads(1, k)
    grads_for(0)
    ghr[pl.ds(t, 1)] = ghs[pl.ds(t, 1)]

    row = Exchange(ms, myr, mzr, mgr)
    row.begin(placing[1], merged)

    for f in range(width // 256):
        gownt[f * 256 : (f + 1) * 256, :] = mm_t(eye, gown[:, f * 256 : (f + 1) * 256]).astype(BF16)
    def terms_b(side):
        def one(c, _):
            at = pl.ds(pl.multiple_of(side * half + c * (half // 2), 64), half // 2)
            to = pl.ds(pl.multiple_of(c * (half // 2), 64), half // 2)
            for q in range(nt):
                ob[pl.ds(side, 1), to, q * 128 : (q + 1) * 128] = mm(
                    gownt[at, :], hm[q, :, :128]
                ).astype(BF16)[None]
            return 0

        lax.fori_loop(0, 2, one, 0)

    def terms_a(side, k):
        cols = pl.ds(pl.multiple_of(side * half, 128), half)
        q = at_t(k)
        value = mm(hmt[pl.ds(q, 1)].reshape(wide, 256), gown[:, cols])
        oa[pl.ds(side, 1), pl.ds(q, 1)] = value.astype(BF16)[None, None]

    terms_b(1 - g)
    b = push_all(obg, [(ob.at[1 - g], obg, dev_g)])
    a = []
    for k in to_t + (0,):
        terms_a(1 - g, k)
        a.append(push_all(oag.at[0], [(oa.at[1 - g, at_t(k)], oag.at[at_t(k)], dev_g)]))
    terms_b(g)

    def spread(j):
        def one(i, _):
            cols = pl.ds(pl.multiple_of(i * 256, 256), 256)
            total = jnp.zeros((prows, 256), F32)
            for p in range(nt):
                order = ones_where(lane_i == 4 * (row_i - 64 * i) + p).astype(BF16)
                total += mm(ghr[p, j * prows : (j + 1) * prows, :], order)
            ght[j * prows : (j + 1) * prows, cols] = total.astype(BF16)
            return 0

        lax.fori_loop(0, images, one, 0, unroll=2)

    def back_head(h):
        row = h * 3 * HEAD_V

        def back_image(i, _):
            cols = pl.ds(pl.multiple_of(i * 256, 256), 256)
            at_q, at_k, at_v = row, row + HEAD_V, row + 2 * HEAD_V
            q_t = qkvt[at_q : at_q + HEAD_V, cols]
            k_t = qkvt[at_k : at_k + HEAD_V, cols]
            v_t = qkvt[at_v : at_v + HEAD_V, cols]
            d_t = ght[h * HEAD_V : (h + 1) * HEAD_V, cols]
            v = mm_t(eye, v_t).astype(BF16)
            weights = probs[i * heads + h]
            grad_v = mm_t(d_t, weights).astype(BF16)
            parts = []
            for c in range(2):
                lanes = slice(c * 128, (c + 1) * 128)
                w = weights[:, lanes].astype(F32)
                grad_w = mm(v, d_t[:, lanes]).astype(BF16).astype(F32)
                inner = jnp.sum(w * grad_w, axis=0, keepdims=True)
                parts.append((w * (grad_w - inner) * HEAD_V**-0.5).astype(BF16))
            grad_s = jnp.concatenate(parts, axis=1)
            grad_q = mm(k_t, grad_s).astype(BF16)
            grad_k = mm_t(q_t, grad_s).astype(BF16)
            qkvt[at_q : at_q + HEAD_V, cols] = grad_q
            qkvt[at_k : at_k + HEAD_V, cols] = grad_k
            qkvt[at_v : at_v + HEAD_V, cols] = grad_v
            return 0

        lax.fori_loop(0, images, back_image, 0, unroll=4)

    def weight_terms(h, side):
        def one(c, _):
            at = pl.ds(pl.multiple_of(side * half + c * (half // 2), 64), half // 2)
            dws[h, at, :] = mm_t(
                nrmt[at, :], qkvt[h * 3 * HEAD_V : (h + 1) * 3 * HEAD_V, :]
            ).astype(BF16)
            return 0

        lax.fori_loop(0, 2, one, 0, unroll=2)

    def to_shards():
        r, c = iota((NZ * 32, yrows), 0), iota((NZ * 32, yrows), 1)
        return ones_where((c == (r >> 5) * zrows + (r & 31)) & ((r & 31) < zrows)).astype(BF16)

    def add(a, b):
        return a.astype(F32) + b.astype(F32)

    their_rows = pl.ds(pl.multiple_of((1 - g) * half, 128), half)
    own_rows = pl.ds(pl.multiple_of(g * half, 128), half)
    order_y = [(k, k - 1) for k in (1, 3, 2)]
    order_z = [(k, k - 1) for k in (4, 3, 5, 2, 6, 1, 7)]

    def rows_y(k):
        return pl.ds(pl.multiple_of(at_y(k) * yrows, 16), yrows)

    def weight_start(h):
        weight_terms(h, 1 - g)
        group = push_all(dgr.at[h], [(dws.at[h, their_rows, :], dgr.at[h], dev_g)])
        weight_terms(h, g)
        return group

    def weight_y(h, group):
        group.arrived()
        dgr[h] = add(dws[h, own_rows, :], dgr[h]).astype(BF16)
        return push_all(
            dyr.at[h], [(dgr.at[h, rows_y(k), :], dyr.at[h, j], dev_y(k)) for k, j in order_y]
        )

    def weight_z(h, group):
        group.arrived()
        total = dgr[h, rows_y(0), :].astype(F32)
        for k in range(1, ny):
            total += dyr[h, k - 1].astype(F32)
        dz[h] = mm(to_shards(), total.astype(BF16)).astype(BF16)
        return push_all(
            dzr.at[h],
            [(dz.at[h, rows(at_z(k) * 32, 32), :], dzr.at[h, j], dev_z(k)) for k, j in order_z],
        )

    def weight_end(h, group):
        group.arrived()
        total = dz[h, rows(z * 32, 32), :].astype(F32)
        for k in range(1, NZ):
            total += dzr[h, k - 1].astype(F32)
        gq_ref[:, h * 3 * HEAD_V : (h + 1) * 3 * HEAD_V] = total[:zrows]

    def b_y(group):
        group.arrived()
        obg[...] = add(ob[pl.ds(g, 1)].reshape(half, nt * 128), obg[...]).astype(BF16)
        return push_all(obyr, [(obg.at[rows_y(k), :], obyr.at[j], dev_y(k)) for k, j in order_y])

    def b_x(group):
        group.arrived()
        total = obg[rows_y(0), :].astype(F32)
        for k in range(1, ny):
            total += obyr[k - 1].astype(F32)
        for q in range(nt):
            obx[q] = total[:, q * 128 : (q + 1) * 128].astype(BF16)
        return push_all(obxr, [(obx.at[at_t(k)], obxr.at[k - 1], dev_t(k)) for k in to_t])

    def b_z(group):
        group.arrived()
        total = obx[pl.ds(t, 1)].reshape(yrows, 128).astype(F32)
        for k in range(1, nt):
            total += obxr[k - 1].astype(F32)
        obz[...] = mm(to_shards(), total.astype(BF16)).astype(BF16)
        return push_all(
            obzr, [(obz.at[rows(at_z(k) * 32, 32), :], obzr.at[j], dev_z(k)) for k, j in order_z]
        )

    def b_end(group):
        group.arrived()
        total = obz[rows(z * 32, 32), :].astype(F32)
        for k in range(1, NZ):
            total += obzr[k - 1].astype(F32)
        go_ref[:, :128] = total[:zrows]

    def a_x(groups):
        out = Group(oax)
        for k, group in zip(to_t + (0,), groups):
            group.arrived()
            q = at_t(k)
            mine = oa[pl.ds(g, 1), pl.ds(q, 1)].reshape(wide, half)
            oag[pl.ds(q, 1)] = add(mine, oag[pl.ds(q, 1)].reshape(wide, half)).astype(BF16)[None]
            if k:
                out.push(oag.at[q], oax.at[k - 1], dev_t(k))
        return out

    def a_y(group):
        group.arrived()
        for f in range(half // 128):
            cols = slice(f * 128, (f + 1) * 128)
            total = oag[pl.ds(t, 1), :, cols].reshape(wide, 128).astype(F32)
            for k in range(1, nt):
                total += oax[k - 1, :, cols].astype(F32)
            oay[cols, :] = mm_t(eye[:128, :128], total.astype(BF16)).astype(BF16)
        return push_all(oayr, [(oay.at[rows_y(k), :], oayr.at[j], dev_y(k)) for k, j in order_y])

    def a_z(group):
        group.arrived()
        total = oay[rows_y(0), :].astype(F32)
        for k in range(1, ny):
            total += oayr[k - 1].astype(F32)
        oaz[...] = mm(to_shards(), total.astype(BF16)).astype(BF16)
        return push_all(
            oazr, [(oaz.at[rows(at_z(k) * 32, 32), :], oazr.at[j], dev_z(k)) for k, j in order_z]
        )

    def a_end(group):
        group.arrived()
        total = oaz[rows(z * 32, 32), :].astype(F32)
        for k in range(1, NZ):
            total += oazr[k - 1].astype(F32)
        go_ref[:, 128:] = total[:zrows]

    b = b_y(b)
    for k in to_t + (0,):
        terms_a(g, k)
    grads_in[0].arrived()
    spread(0)
    back_head(0)
    a = a_x(a)
    w0 = weight_start(0)
    row.second(1)
    back_head(1)
    w0 = weight_y(0, w0)
    row.second(0)
    w1 = weight_start(1)
    grads_in[1].arrived()
    spread(1)
    b = b_x(b)
    back_head(2)
    w1 = weight_y(1, w1)
    w2 = weight_start(2)
    w0 = weight_z(0, w0)
    b = b_z(b)
    a = a_y(a)
    back_head(3)
    w2 = weight_y(2, w2)
    w1 = weight_z(1, w1)
    w3 = weight_start(3)
    row.third(0)
    a = a_z(a)
    w3 = weight_y(3, w3)
    row.third(1)
    w2 = weight_z(2, w2)
    weight_end(0, w0)
    b_end(b)
    weight_end(1, w1)
    w3 = weight_z(3, w3)
    row.end(returning[...], image)
    store_i = pltpu.make_async_copy(image, image_hbm, lsem.at[images + 3])
    store_i.start()
    a_end(a)
    weight_end(2, w2)
    weight_end(3, w3)
    store_i.wait()
    for group in list(open_sends.values()):
        group.sent()
    assert used[0] == n_sems


def hand_over(a, b, c, a_out, b_out, c_out):
    a_out[...] = a[...]
    b_out[...] = b[...]
    c_out[...] = c[...]


def shards(
    ny, nt, patches_in, gain_attn, gain_merge, qkv_weight, out_weight, cotangent, patch_counts, block_target
):
    row_count, width = patches_in.shape
    images = patch_counts.shape[0]
    hcols = out_weight.shape[0]
    heads = hcols // HEAD_V
    cols = 3 * HEAD_V
    half, yrows = width // 2, width // 2 // ny
    wide = hcols - 128
    zrows = yrows // NZ
    n_sems = 3 + 2 + 1 + 6 + 6 + 2 + 4 + (nt + 3) + 3 * heads
    v = pltpu.VMEM
    scratch = [
        v((row_count, width), BF16),
        v((3 * hcols, width), BF16),
        v((256, width), BF16),
        v((256, width), BF16),
        v((width, row_count), BF16),
        v((3 * hcols, row_count), BF16),
        v((images * heads, 256, 256), BF16),
        v((hcols, 256), BF16),
        v((images, 256, hcols), BF16),
        v((nt, 256, hcols), BF16),
        v((nt, hcols, width), BF16),
        v((256, width), F32),
        v((8, 128), I32),
        v((ny, 8, 128), I32),
        v((NZ, ny, 8, 128), I32),
        v((2, NZ, ny, 8, 128), I32),
        v((2, 256, 256), BF16),
        v((256, 256), BF16),
        v((2, 256, half), BF16),
        v((2, ny, 64, half), BF16),
        v((2, NZ, 32, half), BF16),
        v((2, 2, 128, half), BF16),
        v((2, 256, half), BF16),
        v((2, ny, 64, half), BF16),
        v((2, NZ, 32, half), BF16),
        v((2, 2, 128, half), BF16),
        v((256, width), BF16),
        v((256, width), BF16),
        v((256, width), BF16),
        v((256, width), BF16),
        v((width, 256), BF16),
        v((nt, wide, 256), BF16),
        v((nt, hcols, 256), BF16),
        v((nt, hcols, 256), BF16),
        v((hcols, row_count), BF16),
        v((2, nt, wide, half), BF16),
        v((nt, wide, half), BF16),
        v((nt - 1, wide, half), BF16),
        v((half, wide), BF16),
        v((ny - 1, yrows, wide), BF16),
        v((NZ * 32, wide), BF16),
        v((NZ - 1, 32, wide), BF16),
        v((2, half, nt * 128), BF16),
        v((half, nt * 128), BF16),
        v((ny - 1, yrows, nt * 128), BF16),
        v((nt, yrows, 128), BF16),
        v((nt - 1, yrows, 128), BF16),
        v((NZ * 32, 128), BF16),
        v((NZ - 1, 32, 128), BF16),
        v((heads, width, cols), BF16),
        v((heads, half, cols), BF16),
        v((heads, ny - 1, yrows, cols), BF16),
        v((heads, NZ * 32, cols), BF16),
        v((heads, NZ - 1, 32, cols), BF16),
        pltpu.SemaphoreType.DMA((images + 4,)),
        pltpu.SemaphoreType.DMA((n_sems,)),
        pltpu.SemaphoreType.DMA((n_sems,)),
    ]
    in_vmem = pl.BlockSpec(memory_space=pltpu.VMEM)
    in_hbm = pl.BlockSpec(memory_space=pl.ANY)
    image_rows, gq, go = pl.pallas_call(
        functools.partial(kernel, ny, nt, n_sems),
        out_shape=(
            jax.ShapeDtypeStruct((256, width), BF16),
            jax.ShapeDtypeStruct((zrows, heads * cols), F32),
            jax.ShapeDtypeStruct((zrows, hcols), F32),
        ),
        in_specs=[pl.BlockSpec(memory_space=pltpu.SMEM)] + [in_vmem] * 3 + [in_hbm] * 4,
        out_specs=(in_hbm, in_vmem, in_vmem),
        scratch_shapes=scratch,
        compiler_params=pltpu.CompilerParams(
            collective_id=0, has_side_effects=True, vmem_limit_bytes=62 << 20
        ),
        name="block",
    )(
        patch_counts,
        gain_attn,
        gain_merge,
        block_target.reshape(1, -1),
        patches_in,
        qkv_weight.T,
        out_weight,
        cotangent,
    )
    image_rows, grad_qkv, grad_out = pl.pallas_call(
        hand_over,
        out_shape=tuple(jax.ShapeDtypeStruct(a.shape, a.dtype) for a in (image_rows, gq, go)),
        in_specs=[in_vmem] * 3,
        out_specs=(in_vmem,) * 3,
        name="hand_over",
    )(image_rows, gq, go)
    return image_rows, grad_qkv, grad_out.T


def solution(mesh):
    ny, nt = mesh.shape["seq"] // NZ, mesh.shape["tp"]
    return jax.shard_map(
        functools.partial(shards, ny, nt),
        mesh=mesh,
        in_specs=(
            P(("grp", "seq"), None),
            P(),
            P(),
            P(None, "tp"),
            P("tp", None),
            P(("grp", "seq"), "tp"),
            P(("grp", "seq")),
            P(("grp", "seq")),
        ),
        out_specs=(P(("grp", "seq"), "tp"), P(("grp", "seq"), "tp"), P("tp", ("grp", "seq"))),
        check_vma=False,
    )
```
